128 devices in a mesh: region: 4 (over y_lo, core), shell: 32 (over z, x, y_hi).
Axes of the slice: x: 4, y: 4 (y_hi: 2, y_lo: 2; y = y_hi * 2 + y_lo), z: 4, core: 2. Of those that a mesh axis runs over, the one named last changes fastest.
Arguments:
- features: bfloat16 [256, 64, 2048], P('region', None, 'shell'), may hold values from -6 to 6
- tiles: bfloat16 [256, 64, 576], P('region'), may hold values from -0.125 to 0.125
- neighbours: int32 [256, 8], P('region'), may hold values from 0 to 79, as said below
- rim_blocks: int32 [8, 8], P('region'), may hold values from 0 to 63, as said below
- theta: bfloat16 [2, 4, 32, 32], replicated, may hold values from -0.5 to 0.5
- bias: float32 [2, 32], replicated, may hold values from -3 to 3
- mix: bfloat16 [2, 64, 64], replicated, may hold values from -0.75 to 0.75
Outputs:
- mapped: bfloat16 [256, 64, 2048], P('region', None, 'shell')
The draws below stay inside these ranges and needn't reach their ends.
Inputs may be any that keep to these rules, and one draw needn't show every extreme that they name: `neighbours`: in every region each received position, 0 to 7 and 72 to 79, is named by some block. `rim_blocks`: entries of a row are all different; rows for the region below hold block 0 and local blocks under 64 // 2, rows for the region above hold block 63 and blocks from 32 on.
All inputs are finite; a program needn't handle non-finite values.
Results may differ from the reference program's by a relative error of at most 0.017.
Values may be sent and summed in bfloat16 or wider, within the bound.
A program may use at most 128 MiB of HBM per device.

```python
import math
import jax
import jax.numpy as jnp
from jax import lax

SHELLS = 64
C = 32
BLOCK_PIXELS = 64
NEIGHBOUR_BLOCKS = 8
OPERATOR_TILES = 9
ORDERS = 4
LAYERS = 2
BLOCKS_DEV = 64
RIM = 8
PIXEL_BLOCKS = 256
N_REGION = 4


def draw_neighbours(key, part):
    key_local, key_wide, key_halo = jax.random.split(key, 3)
    extent = BLOCKS_DEV + 2 * RIM
    rows = jnp.arange(BLOCKS_DEV, dtype=jnp.int32)
    offsets = jax.random.randint(key_local, (N_REGION, BLOCKS_DEV, NEIGHBOUR_BLOCKS - 2), -8, 9)
    local = RIM + jnp.clip(rows[None, :, None] + offsets, 0, BLOCKS_DEV - 1)
    wide = jax.random.randint(key_wide, (N_REGION, BLOCKS_DEV, 2), 0, extent)
    orders = jax.vmap(lambda k: jax.random.permutation(k, 2 * RIM))(jax.random.split(key_halo, N_REGION))
    received = jnp.where(orders < RIM, orders, orders + BLOCKS_DEV).astype(jnp.int32)
    last = wide[:, :, 1].at[:, :2 * RIM].set(received)
    joined = jnp.concatenate([local, wide[:, :, :1], last[:, :, None]], axis=2)
    return joined.reshape(N_REGION * BLOCKS_DEV, NEIGHBOUR_BLOCKS).astype(jnp.int32)


def draw_rim_blocks(key, part):
    half = BLOCKS_DEV // 2
    keys = jax.random.split(key, 2 * N_REGION)

    def pick(one_key):
        chosen = (jax.random.permutation(one_key, half - 1) + 1)[:RIM - 1].astype(jnp.int32)
        return jnp.concatenate([jnp.zeros((1,), jnp.int32), chosen])
    picked = jax.vmap(pick)(keys).reshape(N_REGION, 2, RIM)
    picked = picked.at[:, 1, :].set(BLOCKS_DEV - 1 - picked[:, 1, :])
    return picked.reshape(2 * N_REGION, RIM).astype(jnp.int32)


def block_levels(own_key, shape, pieces, low, high):
    gain, own = 1.0, jax.random.fold_in(own_key, 6)
    for dim, parts in pieces:
        draws = jnp.exp(jax.random.uniform(jax.random.fold_in(own, dim), (parts,), jnp.float32, low / len(pieces), high / len(pieces)))
        gain = gain * jnp.repeat(draws, shape[dim] // parts).reshape([-1 if axis == dim else 1 for axis in range(len(shape))])
    return gain


def gaussian(stream_key, shape, scale, limit, cuts=(), kind=jnp.bfloat16):
    drawn = scale * jax.random.normal(stream_key, shape, jnp.float32)
    if cuts:
        drawn = drawn * block_levels(stream_key, shape, cuts, -0.22, 0.18)
    return jnp.clip(drawn, -limit, limit).astype(kind)


def setup_inputs(seed: int = 0) -> dict:
    arg_keys = jax.random.split(jax.random.key(seed), 8)
    features = gaussian(arg_keys[0], (PIXEL_BLOCKS, BLOCK_PIXELS, SHELLS * C), 1.0, 6.0, ((0, 4), (2, 32)))
    tiles = gaussian(arg_keys[1], (PIXEL_BLOCKS, BLOCK_PIXELS, OPERATOR_TILES * BLOCK_PIXELS), (4 * OPERATOR_TILES * BLOCK_PIXELS) ** -0.5, 0.125, ((0, 4),))
    neighbours = draw_neighbours(jax.random.fold_in(arg_keys[7], 71), 0)
    rim_blocks = draw_rim_blocks(jax.random.fold_in(arg_keys[7], 71), 0)
    theta = gaussian(arg_keys[4], (LAYERS, ORDERS, C, C), (ORDERS * C) ** -0.5, 0.5)
    bias = gaussian(arg_keys[5], (LAYERS, C), 0.5, 3.0, (), jnp.float32)
    mix = gaussian(arg_keys[6], (LAYERS, SHELLS, SHELLS), SHELLS ** -0.5, 0.75)
    return dict(features=features, tiles=tiles, neighbours=neighbours, rim_blocks=rim_blocks, theta=theta, bias=bias, mix=mix)


def block_table(neighbours, rim_blocks):
    total_blocks = N_REGION * BLOCKS_DEV
    rims = rim_blocks.reshape(N_REGION, 2, RIM).astype(jnp.int32)
    before = jnp.roll(rims, 1, axis=0)
    after = jnp.roll(rims, -1, axis=0)
    base = jnp.arange(N_REGION, dtype=jnp.int32) * BLOCKS_DEV
    lower_base = (base - BLOCKS_DEV) % total_blocks
    upper_base = (base + BLOCKS_DEV) % total_blocks
    own_rows = base[:, None] + jnp.arange(BLOCKS_DEV, dtype=jnp.int32)[None, :]
    neighbour_table = jnp.concatenate([lower_base[:, None] + before[:, 1, :], own_rows, upper_base[:, None] + after[:, 0, :]], axis=1).astype(jnp.int32)
    local = neighbours.reshape(N_REGION, BLOCKS_DEV, NEIGHBOUR_BLOCKS).astype(jnp.int32)
    found = jax.vmap(lambda row, index: row[index])(neighbour_table, local)
    return found.reshape(total_blocks, NEIGHBOUR_BLOCKS).astype(jnp.int32)


def laplace(sky_field, tiles, neighbour_table):
    total_blocks = sky_field.shape[0]
    feature_width = sky_field.shape[2]
    shell_group = math.gcd(total_blocks, 32)
    item_count = total_blocks // shell_group

    def single_item(items):
        tile, index, own_block = items
        nearby_blocks = sky_field[index]
        stacked_terms = jnp.concatenate([own_block[:, None], nearby_blocks], axis=1).reshape(shell_group, OPERATOR_TILES * BLOCK_PIXELS, feature_width)
        return jnp.einsum('bpq,bqf->bpf', tile.astype(jnp.float32), stacked_terms.astype(jnp.float32))

    result_value = lax.map(single_item, (tiles.reshape(item_count, shell_group, BLOCK_PIXELS, OPERATOR_TILES * BLOCK_PIXELS), neighbour_table.reshape(item_count, shell_group, NEIGHBOUR_BLOCKS), sky_field.reshape(item_count, shell_group, BLOCK_PIXELS, feature_width)))
    return result_value.reshape(total_blocks, BLOCK_PIXELS, feature_width)


def reference(features, tiles, neighbours, rim_blocks, theta, bias, mix):
    total_blocks = N_REGION * BLOCKS_DEV
    neighbour_table = block_table(neighbours, rim_blocks)
    state = features
    for layer in range(LAYERS):
        inner = state
        first = laplace(inner, tiles, neighbour_table).astype(jnp.bfloat16)
        second = (2.0 * laplace(first, tiles, neighbour_table) - inner.astype(jnp.float32)).astype(jnp.bfloat16)
        third = (2.0 * laplace(second, tiles, neighbour_table) - first.astype(jnp.float32)).astype(jnp.bfloat16)
        summed = jnp.zeros((total_blocks * BLOCK_PIXELS * SHELLS, C), jnp.float32)
        for order, term in enumerate([inner, first, second, third]):
            summed = summed + jnp.dot(term.reshape(-1, C), theta[layer, order], preferred_element_type=jnp.float32)
        act = jax.nn.relu(summed + bias[layer].astype(jnp.float32)[None, :]).astype(jnp.bfloat16)
        act = act.reshape(total_blocks, BLOCK_PIXELS, SHELLS, C)
        mixed = jnp.einsum('ts,bpsc->bptc', mix[layer].astype(jnp.float32), act.astype(jnp.float32))
        state = mixed.astype(jnp.bfloat16).reshape(total_blocks, BLOCK_PIXELS, SHELLS * C)
    return state
```

```python
import jax
import jax.numpy as jnp
from jax import lax
from jax.sharding import PartitionSpec as P


def from_behind(value, axis, by):
    length = lax.axis_size(axis)
    return lax.ppermute(value, axis, [(i, (i + by) % length) for i in range(length)])


def apply_operator(sky_field, own_tiles, far_tiles, neighbours, rim_blocks):
    lower = sky_field[rim_blocks[0]]
    upper = sky_field[rim_blocks[1]]
    below = from_behind(upper, "region", 1)
    above = from_behind(lower, "region", -1)
    extended = jnp.concatenate([below, sky_field, above], axis=0)
    nearby_blocks = extended[neighbours]
    own_term = jnp.einsum("bpq,bqf->bpf", own_tiles, sky_field, preferred_element_type=jnp.float32)
    far_term = jnp.einsum(
        "bpjq,bjqf->bpf", far_tiles, nearby_blocks, preferred_element_type=jnp.float32
    )
    return own_term + far_term


def mix_shells(weights, value):
    return jnp.einsum("ts,bpsc->bptc", weights, value, preferred_element_type=jnp.float32)


def filtered(state, theta, own_tiles, far_tiles, neighbours, rim_blocks):
    blocks, block_size, feature_width = state.shape
    channels = theta.shape[1]
    inner = state
    first = apply_operator(inner, own_tiles, far_tiles, neighbours, rim_blocks).astype(jnp.bfloat16)
    second = (
        2.0 * apply_operator(first, own_tiles, far_tiles, neighbours, rim_blocks)
        - inner.astype(jnp.float32)
    ).astype(jnp.bfloat16)
    third = (
        2.0 * apply_operator(second, own_tiles, far_tiles, neighbours, rim_blocks)
        - first.astype(jnp.float32)
    ).astype(jnp.bfloat16)
    summed = jnp.zeros((blocks * block_size * feature_width // channels, channels), jnp.float32)
    for order, term in enumerate([inner, first, second, third]):
        summed = summed + jnp.dot(
            term.reshape(-1, channels), theta[order], preferred_element_type=jnp.float32
        )
    return summed


def on_device(features, tiles, neighbours, rim_blocks, theta, bias, mix):
    blocks, block_size, feature_width = features.shape
    channels = theta.shape[2]
    own_tiles = tiles[:, :, :block_size]
    far_tiles = tiles[:, :, block_size:].reshape(blocks, block_size, -1, block_size)
    operator = (own_tiles, far_tiles, neighbours, rim_blocks)
    layers = theta.shape[0]
    summed = filtered(features, theta[0], *operator)
    act = jax.nn.relu(summed + bias[0][None, :]).astype(jnp.bfloat16)
    act = act.reshape(blocks, block_size, feature_width)
    summed = filtered(act, theta[1], *operator).astype(jnp.bfloat16)
    summed = summed.reshape(blocks, block_size, feature_width)
    piece = lax.all_to_all(summed, "shell", split_axis=0, concat_axis=2, tiled=True)
    rows, count, full_width = piece.shape
    shaped = piece.reshape(rows, count, mix.shape[1], channels)
    act = jax.nn.relu(mix_shells(mix[0], shaped) + bias[1]).astype(jnp.bfloat16)
    mapped = mix_shells(mix[1], act).astype(jnp.bfloat16)
    return lax.all_to_all(
        mapped.reshape(rows, count, full_width), "shell", split_axis=2, concat_axis=0, tiled=True
    )


def solution(mesh):
    in_specs = (
        P("region", None, "shell"),
        P("region", None, None),
        P("region", None),
        P("region", None),
        P(),
        P(),
        P(),
    )
    out_specs = P("region", None, "shell")
    return jax.shard_map(
        on_device, mesh=mesh, in_specs=in_specs, out_specs=out_specs, check_vma=False
    )
```

```python
import functools

import jax
import jax.numpy as jnp
from jax import lax
from jax.experimental import pallas as pl
from jax.experimental.pallas import tpu as pltpu
from jax.sharding import PartitionSpec as P

MESH = pl.DeviceIdType.MESH
BF16 = jnp.bfloat16
F32 = jnp.float32
GROUP = 8


def dot(a, b):
    return jnp.dot(a, b, preferred_element_type=F32)


def main_kernel(
    near, perm, feat, tiles, w0, w1, b0, b1, mix, landed,
    e0, e1, e2, e3, e4, e5, stage, arrived, mixed_out, back, big,
    rim_send, rim_recv, a2a_send, a2a_recv, *, unroll,
):
    n_shell = lax.axis_size("shell")
    n_region = lax.axis_size("region")
    ext = (e0, e1, e2, e3, e4, e5)
    blocks = feat.shape[0]
    rim = (e0.shape[0] - blocks) // 2
    me = lax.axis_index("shell")
    region = lax.axis_index("region")
    up = lax.rem(region + 1, n_region)
    down = lax.rem(region + n_region - 1, n_region)

    barrier = pltpu.get_barrier_semaphore()

    def greet(k, _):
        pl.semaphore_signal(
            barrier, inc=1, device_id={"shell": lax.rem(me + k, n_shell)}, device_id_type=MESH
        )
        return 0

    lax.fori_loop(1, n_shell, greet, 0)
    for other in (up, down):
        pl.semaphore_signal(barrier, inc=1, device_id={"region": other}, device_id_type=MESH)

    def load_block(i, _):
        e0[i] = feat[perm[i]]
        return 0

    lax.fori_loop(0, blocks, load_block, 0, unroll=8)
    pl.semaphore_wait(barrier, n_shell + 1)

    def rim_copies(k):
        low = pltpu.make_async_remote_copy(
            src_ref=ext[k].at[pl.ds(0, rim)],
            dst_ref=ext[k].at[pl.ds(blocks + rim, rim)],
            send_sem=rim_send.at[k, 0], recv_sem=rim_recv.at[k, 0],
            device_id={"region": down}, device_id_type=MESH,
        )
        high = pltpu.make_async_remote_copy(
            src_ref=ext[k].at[pl.ds(rim, rim)],
            dst_ref=ext[k].at[pl.ds(blocks, rim)],
            send_sem=rim_send.at[k, 1], recv_sem=rim_recv.at[k, 1],
            device_id={"region": up}, device_id_type=MESH,
        )
        return low, high

    def product(k, i):
        parts = [ext[k][i]] + [ext[k][near[i * 8 + j]] for j in range(8)]
        return dot(tiles[perm[i]], jnp.concatenate(parts, axis=0))

    def step(layer, order, i):
        k = 3 * layer + order
        value = product(k, i)
        if order == 0:
            return value.astype(BF16)
        return (2.0 * value - ext[k - 1][i].astype(F32)).astype(BF16)

    def stacked(layer, i, third):
        return jnp.concatenate(
            [ext[3 * layer][i], ext[3 * layer + 1][i], ext[3 * layer + 2][i], third], axis=1
        )

    for copy in rim_copies(0):
        copy.start()
    for k in range(6):
        layer, order = divmod(k, 3)
        for copy in rim_copies(k):
            copy.wait()
        if k < 5:

            def body(i, _):
                value = step(layer, order, i)
                if order == 2:
                    value = jnp.maximum(dot(stacked(layer, i, value), w0[...]) + b0[...], 0.0).astype(BF16)
                ext[k + 1][i] = value
                return 0

            lax.fori_loop(0, 2 * rim, body, 0, unroll=2 * rim)
            for copy in rim_copies(k + 1):
                copy.start()
            lax.fori_loop(2 * rim, blocks, body, 0, unroll=unroll)
        else:

            def last(t, _):
                d = lax.rem(me + t, n_shell)
                pair = jnp.concatenate(
                    [stacked(layer, 2 * d + p, step(layer, order, 2 * d + p)) for p in range(2)], axis=0
                )
                stage[d] = lax.dot_general(
                    w1[...], pair, (((1,), (1,)), ((), ())), preferred_element_type=F32
                ).astype(BF16)
                return 0

            lax.fori_loop(0, n_shell, last, 0, unroll=unroll // 2)

    def exchange(source, target, slot):
        def send(t, _):
            d = lax.rem(me + t, n_shell)
            pltpu.make_async_remote_copy(
                src_ref=source.at[d], dst_ref=target.at[me],
                send_sem=a2a_send.at[slot], recv_sem=a2a_recv.at[slot],
                device_id={"shell": d}, device_id_type=MESH,
            ).start()
            return 0

        lax.fori_loop(1, n_shell, send, 0)
        target[me] = source[me]

    def finish(target, slot):
        all_but_one = target.at[pl.ds(0, n_shell - 1)]
        pltpu.make_async_copy(all_but_one, all_but_one, a2a_send.at[slot]).wait()
        pltpu.make_async_copy(all_but_one, all_but_one, a2a_recv.at[slot]).wait()

    exchange(stage, arrived, 0)

    size = big.shape[1]
    shells = mix.shape[1]
    spread = (
        lax.broadcasted_iota(jnp.int32, (size, shells), 0) // GROUP
        == lax.broadcasted_iota(jnp.int32, (size, shells), 1)
    ).astype(F32).astype(BF16)
    same = (
        lax.broadcasted_iota(jnp.int32, (size, size), 0) % GROUP
        == lax.broadcasted_iota(jnp.int32, (size, size), 1) % GROUP
    )
    for layer in range(2):
        rows = dot(spread, mix[layer]).astype(BF16)
        full = lax.dot_general(rows, spread, (((1,), (1,)), ((), ())), preferred_element_type=F32)
        big[layer] = jnp.where(same, full, 0.0).astype(BF16)

    finish(arrived, 0)
    groups = arrived.shape[1] // (2 * GROUP)
    for g in range(groups):
        rows = pl.ds(g * 2 * GROUP, 2 * GROUP)
        x = arrived[:, rows, :].reshape(size, -1)
        act = jnp.maximum(dot(big[0], x) + b1[:, g : g + 1], 0.0).astype(BF16)
        y = dot(big[1], act).astype(BF16)
        mixed_out[:, rows, :] = y.reshape(n_shell, 2 * GROUP, -1)
    exchange(mixed_out, back, 1)
    finish(back, 1)
    landed[...] = back[...]


def final_kernel(perm, landed, out):
    def body(d, _):
        piece = landed[d].astype(F32)
        groups = piece.shape[0] // (2 * GROUP)
        rows = [
            piece[(2 * g + s) * GROUP : (2 * g + s + 1) * GROUP] for s in range(2) for g in range(groups)
        ]
        turned = jnp.concatenate(rows, axis=0).T.astype(BF16)
        half = turned.shape[0] // 2
        out[perm[2 * d]] = turned[:half]
        out[perm[2 * d + 1]] = turned[half:]
        return 0

    lax.fori_loop(0, landed.shape[0], body, 0, unroll=8)


def renumbering(neighbours, rim_blocks, blocks):
    rims = rim_blocks.reshape(-1)
    ids = jnp.arange(blocks, dtype=jnp.int32)
    match = ids[:, None] == rims[None, :]
    is_rim = jnp.any(match, axis=1)
    free = jnp.where(is_rim, 0, 1)
    before = jnp.sum(jnp.where(ids[None, :] < ids[:, None], free[None, :], 0), axis=1)
    rim_rank = jnp.sum(jnp.where(match, jnp.arange(rims.shape[0], dtype=jnp.int32)[None, :], 0), axis=1)
    position = jnp.where(is_rim, rim_rank, rims.shape[0] + before)
    hits = position[:, None] == ids[None, :]
    perm = jnp.sum(jnp.where(hits, ids[:, None], 0), axis=0)
    half = rims.shape[0] // 2
    edge = jnp.arange(half, dtype=jnp.int32)
    table = jnp.concatenate([blocks + edge, position, blocks + half + edge])
    near = table[neighbours[perm]]
    return near.reshape(-1), perm


def on_device(features, tiles, neighbours, rim_blocks, theta, bias, mix):
    blocks, pixels, width = features.shape
    layers, orders, channels, _ = theta.shape
    shells = mix.shape[1]
    n_shell = lax.axis_size("shell")
    groups = channels // GROUP
    near, perm = renumbering(neighbours, rim_blocks, blocks)
    eye = jnp.eye(2, dtype=BF16)
    w0 = jnp.einsum("kio,st->ksito", theta[0], eye).reshape(orders * width, width)
    w1 = jnp.einsum("kigo,st->gtoksi", theta[1].reshape(orders, channels, groups, GROUP), eye)
    w1 = w1.reshape(width, orders * width)
    b0 = jnp.tile(bias[0], 2)[None, :]
    b1 = jnp.tile(bias[1].reshape(groups, GROUP).T, (shells, 1))
    smem = pl.BlockSpec(memory_space=pltpu.SMEM)
    vmem = pl.BlockSpec(memory_space=pltpu.VMEM)
    rim = rim_blocks.shape[1]
    piece = (n_shell, width, 2 * pixels)
    landed = pl.pallas_call(
        functools.partial(main_kernel, unroll=16),
        out_shape=jax.ShapeDtypeStruct(piece, BF16),
        in_specs=[smem, smem] + [vmem] * 7,
        out_specs=vmem,
        scratch_shapes=[
            *[pltpu.VMEM((blocks + 2 * rim, pixels, width), BF16) for _ in range(6)],
            pltpu.VMEM(piece, BF16),
            pltpu.VMEM(piece, BF16),
            pltpu.VMEM(piece, BF16),
            pltpu.VMEM(piece, BF16),
            pltpu.VMEM((2, shells * GROUP, shells * GROUP), BF16),
            pltpu.SemaphoreType.DMA((6, 2)),
            pltpu.SemaphoreType.DMA((6, 2)),
            pltpu.SemaphoreType.DMA((2,)),
            pltpu.SemaphoreType.DMA((2,)),
        ],
        compiler_params=pltpu.CompilerParams(
            collective_id=0, has_side_effects=True, vmem_limit_bytes=56 * 1024 * 1024
        ),
        name="filter_and_mix",
    )(near, perm, features, tiles, w0, w1, b0, b1, mix)
    return pl.pallas_call(
        final_kernel,
        out_shape=jax.ShapeDtypeStruct(features.shape, BF16),
        in_specs=[smem, vmem],
        out_specs=vmem,
        compiler_params=pltpu.CompilerParams(vmem_limit_bytes=32 * 1024 * 1024),
        name="unpack",
    )(perm, landed)


def solution(mesh):
    in_specs = (
        P("region", None, "shell"),
        P("region", None, None),
        P("region", None),
        P("region", None),
        P(),
        P(),
        P(),
    )
    return jax.shard_map(
        on_device, mesh=mesh, in_specs=in_specs, out_specs=P("region", None, "shell"), check_vma=False
    )
```

```python
import functools

import jax
import jax.numpy as jnp
from jax import lax
from jax.experimental import pallas as pl
from jax.experimental.pallas import tpu as pltpu
from jax.sharding import PartitionSpec as P

MESH = pl.DeviceIdType.MESH
BF16 = jnp.bfloat16
F32 = jnp.float32
I32 = jnp.int32
GROUP = 8
LANES = 128


def dot(a, b):
    return jnp.dot(a, b, preferred_element_type=F32)


def dot_nt(a, b):
    return lax.dot_general(a, b, (((1,), (1,)), ((), ())), preferred_element_type=F32)


def iota(shape, axis):
    return lax.broadcasted_iota(I32, shape, axis)


def number_blocks(near_in, rims, odd, blocks, rim):
    lane = iota((8, LANES), 1)
    rank = jnp.zeros((8, LANES), I32)
    is_rim = jnp.zeros((8, LANES), jnp.bool_)
    for row in range(2):
        first = jnp.where(odd == row, 0, rim)
        for j in range(rim):
            hit = lane == rims[row, j] + rim
            rank = rank + jnp.where(hit, first + j, 0)
            is_rim = is_rim | hit
    own = (lane >= rim) & (lane < blocks + rim)
    free = jnp.where(own & ~is_rim, 1.0, 0.0).astype(BF16)
    earlier = jnp.where(iota((LANES, LANES), 0) < iota((LANES, LANES), 1), 1.0, 0.0).astype(BF16)
    before = dot(free, earlier).astype(I32)
    position = jnp.where(is_rim, rank, 2 * rim + before)
    edge = jnp.where(lane < rim, blocks + lane + rim * odd, lane - rim * odd)
    table = jnp.where(own, position, edge)[0:1, :]

    wide = iota((blocks, LANES), 1)
    tall = iota((blocks, LANES), 0)
    table_rows = jnp.broadcast_to(table, (blocks, LANES)).astype(F32)
    found = jnp.where(wide == near_in.shape[1], tall, 0).astype(F32)
    for j in range(near_in.shape[1]):
        picked = jnp.where(near_in[:, j : j + 1] == wide, table_rows, 0.0)
        found = jnp.where(wide == j, jnp.sum(picked, axis=1, keepdims=True), found)
    gap = jnp.zeros((rim, LANES), F32)
    tail = jnp.zeros((LANES - blocks - rim, LANES), F32)
    hits = jnp.where(table == tall, 1.0, 0.0).astype(BF16)
    ordered = dot(hits, jnp.concatenate([gap, found, tail], axis=0).astype(BF16))
    where_to = jnp.sum(jnp.where(wide == tall + rim, table_rows, 0.0), axis=1, keepdims=True)
    numbers = jnp.where(wide == near_in.shape[1] + 1, where_to, ordered).astype(I32)
    top = jnp.where(wide < near_in.shape[1], blocks + 2 * rim - 1, blocks - 1)
    return jnp.clip(numbers, 0, top)


def main_kernel(
    rims, near_in, feat, tiles_hbm, theta, bias, mix, out,
    e0, e1, e2, e3, e4, e5, tiles, numbers_v, numbers, acc, acc_t, w0, w1,
    packed, landing, stage, arrived, mixed_out, back, big, turned,
    tile_sem, number_sem, chip_send, chip_recv, cross_send, cross_recv, a2a_send, a2a_recv,
    *, unroll,
):
    n_shell = lax.axis_size("shell")
    n_region = lax.axis_size("region")
    ext = (e0, e1, e2, e3, e4, e5)
    blocks, pixels, width = feat.shape
    rim = (e0.shape[0] - blocks) // 2
    channels = theta.shape[2]
    groups = channels // GROUP
    listed = near_in.shape[1]
    me = lax.axis_index("shell")
    region = lax.axis_index("region")
    odd = lax.rem(region, 2)
    above = lax.rem(region + 1, n_region)
    below = lax.rem(region + n_region - 1, n_region)
    chip_mate = above + odd * (below - above)
    cross_mate = below + odd * (above - below)

    barrier = pltpu.get_barrier_semaphore()
    for other in (above, below):
        pl.semaphore_signal(barrier, inc=1, device_id={"region": other}, device_id_type=MESH)

    def greet(k, _):
        pl.semaphore_signal(
            barrier, inc=1, device_id={"shell": lax.rem(me + k, n_shell)}, device_id_type=MESH
        )
        return 0

    lax.fori_loop(1, n_shell, greet, 0)
    tile_copy = pltpu.make_async_copy(tiles_hbm, tiles, tile_sem)
    tile_copy.start()

    def pack(k):
        for p in range(rim // 2):
            packed[p] = jnp.concatenate([ext[k][p], ext[k][p + rim // 2]], axis=1)

    def unpack(k):
        for p in range(rim // 2):
            value = landing[k, p]
            ext[k][blocks + p] = value[:, :width]
            ext[k][blocks + rim // 2 + p] = value[:, width:]

    def rim_copies(k):
        cross = pltpu.make_async_remote_copy(
            src_ref=packed, dst_ref=landing.at[k],
            send_sem=cross_send.at[k], recv_sem=cross_recv.at[k],
            device_id={"region": cross_mate}, device_id_type=MESH,
        )
        chip = pltpu.make_async_remote_copy(
            src_ref=ext[k].at[pl.ds(rim, rim)], dst_ref=ext[k].at[pl.ds(blocks + rim, rim)],
            send_sem=chip_send.at[k], recv_sem=chip_recv.at[k],
            device_id={"region": chip_mate}, device_id_type=MESH,
        )
        return cross, chip

    for j in range(rim):
        e0[j] = feat[rims[odd, j]]
        e0[rim + j] = feat[rims[1 - odd, j]]
    pack(0)
    pl.semaphore_wait(barrier, n_shell + 1)
    for copy in rim_copies(0):
        copy.start()

    numbers_v[...] = number_blocks(near_in, rims, odd, blocks, rim)
    number_copy = pltpu.make_async_copy(numbers_v, numbers, number_sem)
    number_copy.start()

    zero = jnp.zeros((channels, channels), F32)
    for k in range(4):
        weight = theta[0, k].astype(F32)
        w0[k] = jnp.concatenate(
            [jnp.concatenate([weight, zero], axis=1), jnp.concatenate([zero, weight], axis=1)], axis=0
        ).astype(BF16)
        weight = theta[1, k].astype(F32).T
        left = jnp.concatenate([weight, zero], axis=1)
        right = jnp.concatenate([zero, weight], axis=1)
        parts = []
        for g in range(groups):
            parts += [left[g * GROUP : (g + 1) * GROUP], right[g * GROUP : (g + 1) * GROUP]]
        w1[k] = jnp.concatenate(parts, axis=0).astype(BF16)
    b0 = jnp.concatenate([bias[0:1, :], bias[0:1, :]], axis=1)

    size = big.shape[1]
    shells = mix.shape[1]

    def build_mix(layer):
        spread = jnp.where(
            iota((size, shells), 0) // GROUP == iota((size, shells), 1), 1.0, 0.0
        ).astype(BF16)
        rows = dot(spread, mix[layer]).astype(BF16)
        same = iota((size, size), 0) % GROUP == iota((size, size), 1) % GROUP
        big[layer] = jnp.where(same, dot_nt(rows, spread), 0.0).astype(BF16)

    number_copy.wait()

    def load_block(i, _):
        e0[i] = feat[numbers[i, listed]]
        return 0

    lax.fori_loop(2 * rim, blocks, load_block, 0, unroll=8)

    def product(k, i):
        parts = [ext[k][i]] + [ext[k][numbers[i, j]] for j in range(listed)]
        return dot(tiles[numbers[i, listed]], jnp.concatenate(parts, axis=0))

    def step(k, i):
        value = product(k, i)
        if k % 3 == 0:
            return value.astype(BF16)
        return (2.0 * value - ext[k - 1][i].astype(F32)).astype(BF16)

    batch = 8

    def filter_rows(orders, fresh):
        def body(q, _):
            rows = pl.ds(q * batch, batch)
            total = b0 if fresh else acc[rows].reshape(batch * pixels, width)
            for k in orders:
                total = total + dot(ext[k][rows].reshape(batch * pixels, width), w0[k])
            acc[rows] = total.reshape(batch, pixels, width)
            return 0

        lax.fori_loop(0, blocks // batch, body, 0)

    def filter_columns(orders, fresh):
        def body(q, _):
            rows = pl.ds(q * 4, 4)
            total = None
            for k in orders:
                term = dot_nt(w1[k], ext[3 + k][rows].reshape(4 * pixels, width))
                total = term if total is None else total + term
            for p in range(2):
                value = total[:, p * LANES : (p + 1) * LANES]
                acc_t[2 * q + p] = value if fresh else acc_t[2 * q + p] + value
            return 0

        lax.fori_loop(0, blocks // 4, body, 0, unroll=4)

    for k in range(6):
        for copy in rim_copies(k):
            copy.wait()
        unpack(k)
        if k == 0:
            tile_copy.wait()
        if k < 5:

            def body(i, _):
                value = step(k, i)
                if k == 2:
                    value = jnp.maximum(acc[i] + dot(value, w0[3]), 0.0).astype(BF16)
                ext[k + 1][i] = value
                return 0

            lax.fori_loop(0, 2 * rim, body, 0, unroll=2 * rim)
            pack(k + 1)
            for copy in rim_copies(k + 1):
                copy.start()
            lax.fori_loop(2 * rim, blocks, body, 0, unroll=unroll)
            if k == 0:
                filter_rows((0, 1), True)
            elif k == 1:
                filter_rows((2,), False)
            elif k == 2:
                build_mix(0)
            elif k == 3:
                filter_columns((0, 1), True)
            elif k == 4:
                filter_columns((2,), False)

    def a2a_send_piece(source, target, d, slot):
        pltpu.make_async_remote_copy(
            src_ref=source.at[d], dst_ref=target.at[me],
            send_sem=a2a_send.at[slot], recv_sem=a2a_recv.at[slot],
            device_id={"shell": d}, device_id_type=MESH,
        ).start()

    def finish(target, slot):
        all_but_one = target.at[pl.ds(0, n_shell - 1)]
        pltpu.make_async_copy(all_but_one, all_but_one, a2a_send.at[slot]).wait()
        pltpu.make_async_copy(all_but_one, all_but_one, a2a_recv.at[slot]).wait()

    def last_piece(d):
        pair = jnp.concatenate([step(5, 2 * d), step(5, 2 * d + 1)], axis=0)
        return (acc_t[d] + dot_nt(w1[3], pair)).astype(BF16)

    width_of_run = 8

    def last_pieces(t, _):
        for p in range(width_of_run):
            d = lax.rem(me + 1 + t * width_of_run + p, n_shell)
            stage[d] = last_piece(d)
        for p in range(width_of_run):
            d = lax.rem(me + 1 + t * width_of_run + p, n_shell)

            @pl.when(d != me)
            def _():
                a2a_send_piece(stage, arrived, d, 0)

        return 0

    lax.fori_loop(0, n_shell // width_of_run, last_pieces, 0)
    arrived[me] = stage[me]
    build_mix(1)
    b1 = jnp.broadcast_to(bias[1:2, :], (LANES, channels)).T
    finish(arrived, 0)

    for g in range(groups):
        rows = pl.ds(g * 2 * GROUP, 2 * GROUP)
        x = arrived[:, rows, :].reshape(size, LANES)
        total = dot(big[0], x).reshape(shells, GROUP, LANES) + b1[g * GROUP : (g + 1) * GROUP][None]
        act = jnp.maximum(total, 0.0).reshape(size, LANES).astype(BF16)
        mixed_out[:, rows, :] = dot(big[1], act).astype(BF16).reshape(n_shell, 2 * GROUP, LANES)

    def send_mixed(t, _):
        a2a_send_piece(mixed_out, back, lax.rem(me + t, n_shell), 1)
        return 0

    lax.fori_loop(1, n_shell, send_mixed, 0)
    back[me] = mixed_out[me]
    finish(back, 1)

    def turn(d, _):
        piece = back[d].astype(F32)
        rows = [
            piece[(2 * g + s) * GROUP : (2 * g + s + 1) * GROUP] for s in range(2) for g in range(groups)
        ]
        value = jnp.concatenate(rows, axis=0).T.astype(BF16)
        turned[2 * d] = value[:pixels]
        turned[2 * d + 1] = value[pixels:]
        return 0

    lax.fori_loop(0, n_shell, turn, 0, unroll=8)

    def place(b, _):
        out[b] = turned[numbers[b, listed + 1]]
        return 0

    lax.fori_loop(0, blocks, place, 0, unroll=8)


def on_device(features, tiles, neighbours, rim_blocks, theta, bias, mix):
    blocks, pixels, width = features.shape
    shells = mix.shape[1]
    n_shell = lax.axis_size("shell")
    smem = pl.BlockSpec(memory_space=pltpu.SMEM)
    vmem = pl.BlockSpec(memory_space=pltpu.VMEM)
    rim = rim_blocks.shape[1]
    piece = (n_shell, width, 2 * pixels)
    orders = theta.shape[1]
    dma = pltpu.SemaphoreType.DMA
    return pl.pallas_call(
        functools.partial(main_kernel, unroll=16),
        out_shape=jax.ShapeDtypeStruct(features.shape, BF16),
        in_specs=[smem, vmem, vmem, pl.BlockSpec(memory_space=pl.ANY), vmem, vmem, vmem],
        out_specs=vmem,
        scratch_shapes=[
            *[pltpu.VMEM((blocks + 2 * rim, pixels, width), BF16) for _ in range(6)],
            pltpu.VMEM(tiles.shape, BF16),
            pltpu.VMEM((blocks, LANES), I32),
            pltpu.SMEM((blocks, LANES), I32),
            pltpu.VMEM((blocks, pixels, width), F32),
            pltpu.VMEM(piece, F32),
            pltpu.VMEM((orders, width, width), BF16),
            pltpu.VMEM((orders, width, width), BF16),
            pltpu.VMEM((rim // 2, pixels, LANES), BF16),
            pltpu.VMEM((6, rim // 2, pixels, LANES), BF16),
            *[pltpu.VMEM(piece, BF16) for _ in range(4)],
            pltpu.VMEM((2, shells * GROUP, shells * GROUP), BF16),
            pltpu.VMEM((blocks, pixels, width), BF16),
            dma, dma,
            *[dma((6,)) for _ in range(4)],
            dma((2,)), dma((2,)),
        ],
        compiler_params=pltpu.CompilerParams(
            collective_id=0, has_side_effects=True, vmem_limit_bytes=56 * 1024 * 1024
        ),
        name="filter_and_mix",
    )(rim_blocks, neighbours, features, tiles, theta, bias, mix)


def solution(mesh):
    in_specs = (
        P("region", None, "shell"),
        P("region", None, None),
        P("region", None),
        P("region", None),
        P(),
        P(),
        P(),
    )
    return jax.shard_map(
        on_device, mesh=mesh, in_specs=in_specs, out_specs=P("region", None, "shell"), check_vma=False
    )
```

```python
import functools

import jax
import jax.numpy as jnp
from jax import lax
from jax.experimental import pallas as pl
from jax.experimental.pallas import tpu as pltpu
from jax.sharding import PartitionSpec as P

MESH = pl.DeviceIdType.MESH
BF16 = jnp.bfloat16
F32 = jnp.float32
I32 = jnp.int32
GROUP = 8
LANES = 128


def dot(a, b):
    return jnp.dot(a, b, preferred_element_type=F32)


def dot_nt(a, b):
    return lax.dot_general(a, b, (((1,), (1,)), ((), ())), preferred_element_type=F32)


def iota(shape, axis):
    return lax.broadcasted_iota(I32, shape, axis)


def number_blocks(near_t, rims, odd, blocks, rim):
    near_in = near_t.astype(F32).T.astype(I32)
    lane = iota((8, LANES), 1)
    rank = jnp.zeros((8, LANES), I32)
    is_rim = jnp.zeros((8, LANES), jnp.bool_)
    for row in range(2):
        first = jnp.where(odd == row, 0, rim)
        for j in range(rim):
            hit = lane == rims[row, j] + rim
            rank = rank + jnp.where(hit, first + j, 0)
            is_rim = is_rim | hit
    own = (lane >= rim) & (lane < blocks + rim)
    free = jnp.where(own & ~is_rim, 1.0, 0.0).astype(BF16)
    earlier = jnp.where(iota((LANES, LANES), 0) < iota((LANES, LANES), 1), 1.0, 0.0).astype(BF16)
    before = dot(free, earlier).astype(I32)
    position = jnp.where(is_rim, rank, 2 * rim + before)
    edge = jnp.where(lane < rim, blocks + lane + rim * odd, lane - rim * odd)
    table = jnp.where(own, position, edge)[0:1, :]

    wide = iota((blocks, LANES), 1)
    tall = iota((blocks, LANES), 0)
    table_rows = jnp.broadcast_to(table, (blocks, LANES)).astype(F32)
    found = jnp.where(wide == near_in.shape[1], tall, 0).astype(F32)
    for j in range(near_in.shape[1]):
        picked = jnp.where(near_in[:, j : j + 1] == wide, table_rows, 0.0)
        found = jnp.where(wide == j, jnp.sum(picked, axis=1, keepdims=True), found)
    gap = jnp.zeros((rim, LANES), F32)
    tail = jnp.zeros((LANES - blocks - rim, LANES), F32)
    hits = jnp.where(table == tall, 1.0, 0.0).astype(BF16)
    ordered = dot(hits, jnp.concatenate([gap, found, tail], axis=0).astype(BF16))
    where_to = jnp.sum(jnp.where(wide == tall + rim, table_rows, 0.0), axis=1, keepdims=True)
    numbers = jnp.where(wide == near_in.shape[1] + 1, where_to, ordered).astype(I32)
    top = jnp.where(wide < near_in.shape[1], blocks + 2 * rim - 1, blocks - 1)
    return jnp.clip(numbers, 0, top)


def main_kernel(
    rims_hbm, near_hbm, feat_hbm, tiles_hbm, theta_hbm, bias_hbm, mix_hbm, landed, numbers_v,
    e0, e1, e2, e3, e4, e5, rims, near_in, feat, tiles, theta, bias, mix, numbers, acc, acc_t, w0, w1,
    packed, landing, stage, arrived, mixed_out, big, third,
    input_sem, number_sem, own_sem, chip_send, chip_recv, cross_send, cross_recv, a2a_send, a2a_recv,
    *, unroll,
):
    n_shell = lax.axis_size("shell")
    n_region = lax.axis_size("region")
    ext = (e0, e1, e2, e3, e4, e5)
    blocks, pixels, width = feat.shape
    rim = (e0.shape[0] - blocks) // 2
    channels = theta.shape[2]
    groups = channels // GROUP
    listed = near_in.shape[0]
    me = lax.axis_index("shell")
    region = lax.axis_index("region")
    odd = lax.rem(region, 2)
    above = lax.rem(region + 1, n_region)
    below = lax.rem(region + n_region - 1, n_region)
    chip_mate = above + odd * (below - above)
    cross_mate = below + odd * (above - below)

    sources = (rims_hbm, feat_hbm, near_hbm, tiles_hbm, theta_hbm, bias_hbm, mix_hbm)
    targets = (rims, feat, near_in, tiles, theta, bias, mix)
    loads = [
        pltpu.make_async_copy(source, target, input_sem.at[n])
        for n, (source, target) in enumerate(zip(sources, targets))
    ]
    loads[0].start()
    loads[1].start()
    barrier = pltpu.get_barrier_semaphore()
    for other in (above, below):
        pl.semaphore_signal(barrier, inc=1, device_id={"region": other}, device_id_type=MESH)
    for load in loads[2:]:
        load.start()

    def greet(k, _):
        pl.semaphore_signal(
            barrier, inc=1, device_id={"shell": lax.rem(me + k, n_shell)}, device_id_type=MESH
        )
        return 0

    lax.fori_loop(1, n_shell, greet, 0)

    def pack(k):
        for p in range(rim // 2):
            packed[p] = jnp.concatenate([ext[k][p], ext[k][p + rim // 2]], axis=1)

    def unpack(k):
        for p in range(rim // 2):
            value = landing[k, p]
            ext[k][blocks + p] = value[:, :width]
            ext[k][blocks + rim // 2 + p] = value[:, width:]

    def rim_copies(k):
        cross = pltpu.make_async_remote_copy(
            src_ref=packed, dst_ref=landing.at[k],
            send_sem=cross_send.at[k], recv_sem=cross_recv.at[k],
            device_id={"region": cross_mate}, device_id_type=MESH,
        )
        chip = pltpu.make_async_remote_copy(
            src_ref=ext[k].at[pl.ds(rim, rim)], dst_ref=ext[k].at[pl.ds(blocks + rim, rim)],
            send_sem=chip_send.at[k], recv_sem=chip_recv.at[k],
            device_id={"region": chip_mate}, device_id_type=MESH,
        )
        return cross, chip

    loads[0].wait()
    loads[1].wait()
    for j in range(rim):
        e0[j] = feat[rims[odd, j]]
        e0[rim + j] = feat[rims[1 - odd, j]]
    pack(0)
    pl.semaphore_wait(barrier, n_shell + 1)
    for copy in rim_copies(0):
        copy.start()

    loads[2].wait()
    numbers_v[...] = number_blocks(near_in[...], rims, odd, blocks, rim)
    number_copy = pltpu.make_async_copy(numbers_v, numbers, number_sem)
    number_copy.start()

    for load in loads[4:]:
        load.wait()
    zero = jnp.zeros((channels, channels), F32)
    for k in range(4):
        weight = theta[0, k].astype(F32)
        w0[k] = jnp.concatenate(
            [jnp.concatenate([weight, zero], axis=1), jnp.concatenate([zero, weight], axis=1)], axis=0
        ).astype(BF16)
        weight = theta[1, k].astype(F32).T
        left = jnp.concatenate([weight, zero], axis=1)
        right = jnp.concatenate([zero, weight], axis=1)
        parts = []
        for g in range(groups):
            parts += [left[g * GROUP : (g + 1) * GROUP], right[g * GROUP : (g + 1) * GROUP]]
        w1[k] = jnp.concatenate(parts, axis=0).astype(BF16)
    b0 = jnp.concatenate([bias[0:1, :], bias[0:1, :]], axis=1)

    size = big.shape[1]
    shells = mix.shape[1]

    spread = jnp.where(
        lax.shift_right_logical(iota((size, shells), 0), 3) == iota((size, shells), 1), 1.0, 0.0
    ).astype(BF16)
    same = jnp.where(
        iota((GROUP, size), 0) == lax.bitwise_and(iota((GROUP, size), 1), GROUP - 1), 1.0, 0.0
    )

    def build_mix(layer):
        rows = dot(spread, mix[layer]).astype(BF16)
        full = dot_nt(rows, spread).reshape(shells, GROUP, size)
        big[layer] = (full * same[None]).reshape(size, size).astype(BF16)

    number_copy.wait()

    def load_block(i, _):
        e0[i] = feat[numbers[i, listed]]
        return 0

    lax.fori_loop(2 * rim, blocks, load_block, 0, unroll=8)

    def product(k, i):
        parts = [ext[k][i]] + [ext[k][numbers[i, j]] for j in range(listed)]
        return dot(tiles[numbers[i, listed]], jnp.concatenate(parts, axis=0))

    def step(k, i):
        value = product(k, i)
        if k % 3 == 0:
            return value.astype(BF16)
        return (2.0 * value - ext[k - 1][i].astype(F32)).astype(BF16)

    batch = 8

    def filter_rows(orders, fresh):
        def body(q, _):
            rows = pl.ds(q * batch, batch)
            total = b0 if fresh else acc[rows].reshape(batch * pixels, width)
            for k in orders:
                total = total + dot(ext[k][rows].reshape(batch * pixels, width), w0[k])
            acc[rows] = total.reshape(batch, pixels, width)
            return 0

        lax.fori_loop(0, blocks // batch, body, 0)

    def filter_columns(orders, fresh):
        def body(q, _):
            rows = pl.ds(q * 4, 4)
            total = None
            for k in orders:
                term = dot_nt(w1[k], ext[3 + k][rows].reshape(4 * pixels, width))
                total = term if total is None else total + term
            for p in range(2):
                value = total[:, p * LANES : (p + 1) * LANES]
                acc_t[2 * q + p] = value if fresh else acc_t[2 * q + p] + value
            return 0

        lax.fori_loop(0, blocks // 4, body, 0, unroll=4)

    def activate(first, end):
        def body(q, _):
            rows = pl.ds(first + q * batch, batch)
            total = acc[rows].reshape(batch * pixels, width)
            total = total + dot(e3[rows].reshape(batch * pixels, width), w0[3])
            e3[rows] = jnp.maximum(total, 0.0).astype(BF16).reshape(batch, pixels, width)
            return 0

        lax.fori_loop(0, (end - first) // batch, body, 0)

    for k in range(6):
        for copy in rim_copies(k):
            copy.wait()
        unpack(k)
        if k == 0:
            loads[3].wait()
        if k < 5:

            def body(i, _):
                ext[k + 1][i] = step(k, i)
                return 0

            lax.fori_loop(0, 2 * rim, body, 0, unroll=2 * rim)
            if k == 2:
                activate(0, 2 * rim)
            pack(k + 1)
            for copy in rim_copies(k + 1):
                copy.start()
            lax.fori_loop(2 * rim, blocks, body, 0, unroll=unroll)
            if k == 2:
                activate(2 * rim, blocks)
            if k == 0:
                filter_rows((0, 1), True)
            elif k == 1:
                filter_rows((2,), False)
            elif k == 2:
                build_mix(0)
            elif k == 3:
                filter_columns((0, 1), True)
            elif k == 4:
                filter_columns((2,), False)

    def a2a_send_piece(source, target, d, slot):
        pltpu.make_async_remote_copy(
            src_ref=source.at[d], dst_ref=target.at[me],
            send_sem=a2a_send.at[slot], recv_sem=a2a_recv.at[slot],
            device_id={"shell": d}, device_id_type=MESH,
        ).start()

    def finish(target, slot):
        all_but_one = target.at[pl.ds(0, n_shell - 1)]
        pltpu.make_async_copy(all_but_one, all_but_one, a2a_send.at[slot]).wait()
        pltpu.make_async_copy(all_but_one, all_but_one, a2a_recv.at[slot]).wait()

    width_of_run = 8

    def last_pieces(t, _):
        for p in range(width_of_run):
            d = lax.rem(me + 1 + t * width_of_run + p, n_shell)
            third[2 * d] = step(5, 2 * d)
            third[2 * d + 1] = step(5, 2 * d + 1)
        for p in range(width_of_run):
            d = lax.rem(me + 1 + t * width_of_run + p, n_shell)
            pair = third[pl.ds(2 * d, 2)].reshape(2 * pixels, width)
            stage[d] = (acc_t[d] + dot_nt(w1[3], pair)).astype(BF16)
        for p in range(width_of_run):
            d = lax.rem(me + 1 + t * width_of_run + p, n_shell)

            @pl.when(d != me)
            def _():
                a2a_send_piece(stage, arrived, d, 0)

        return 0

    lax.fori_loop(0, n_shell // width_of_run, last_pieces, 0)
    arrived[me] = stage[me]
    build_mix(1)
    b1 = jnp.broadcast_to(bias[1:2, :], (LANES, channels)).T
    finish(arrived, 0)

    def rows_of(g):
        return pl.ds(g * 2 * GROUP, 2 * GROUP)

    for g in range(0, groups, 2):
        x = jnp.concatenate([arrived[:, rows_of(g + p), :].reshape(size, LANES) for p in range(2)], axis=1)
        lift = jnp.concatenate([b1[(g + p) * GROUP : (g + p + 1) * GROUP] for p in range(2)], axis=1)
        total = dot(big[0], x).reshape(shells, GROUP, 2 * LANES) + lift[None]
        act = jnp.maximum(total, 0.0).reshape(size, 2 * LANES).astype(BF16)
        y = dot(big[1], act).astype(BF16)
        for p in range(2):
            part = y[:, p * LANES : (p + 1) * LANES]
            mixed_out[:, rows_of(g + p), :] = part.reshape(n_shell, 2 * GROUP, LANES)

    own = pltpu.make_async_copy(mixed_out.at[me], landed.at[me], own_sem)
    own.start()

    def send_mixed(t, _):
        a2a_send_piece(mixed_out, landed, lax.rem(me + t, n_shell), 1)
        return 0

    lax.fori_loop(1, n_shell, send_mixed, 0)
    own.wait()
    finish(landed, 1)


def unpack_kernel(numbers_hbm, landed_hbm, out_hbm, numbers, landed, turned, placed, sem, load_sem, *, slot):
    blocks, pixels, width = out_hbm.shape
    share = landed.shape[0] // 4
    loads = []
    for q in range(4):
        rows = pl.ds(q * share, share)
        loads.append(pltpu.make_async_copy(landed_hbm.at[rows], landed.at[rows], load_sem.at[q]))
        loads[-1].start()
    number_copy = pltpu.make_async_copy(numbers_hbm, numbers, load_sem.at[4])
    number_copy.start()
    groups = width // (2 * GROUP)

    def turn(d, _):
        piece = landed[d].astype(F32)
        rows = [
            piece[(2 * g + s) * GROUP : (2 * g + s + 1) * GROUP] for s in range(2) for g in range(groups)
        ]
        value = jnp.concatenate(rows, axis=0).T.astype(BF16)
        turned[2 * d] = value[:pixels]
        turned[2 * d + 1] = value[pixels:]
        return 0

    for q in range(4):
        loads[q].wait()
        lax.fori_loop(q * share, (q + 1) * share, turn, 0, unroll=8)
    number_copy.wait()
    run = blocks // 4
    copies = []
    for q in range(4):

        def place(b, _):
            placed[b] = turned[numbers[b, slot]]
            return 0

        lax.fori_loop(q * run, (q + 1) * run, place, 0, unroll=8)
        rows = pl.ds(q * run, run)
        copies.append(pltpu.make_async_copy(placed.at[rows], out_hbm.at[rows], sem.at[q]))
        copies[-1].start()
    for copy in copies:
        copy.wait()


def on_device(features, tiles, neighbours, rim_blocks, theta, bias, mix):
    blocks, pixels, width = features.shape
    shells = mix.shape[1]
    n_shell = lax.axis_size("shell")
    vmem = pl.BlockSpec(memory_space=pltpu.VMEM)
    rim = rim_blocks.shape[1]
    piece = (n_shell, width, 2 * pixels)
    orders = theta.shape[1]
    dma = pltpu.SemaphoreType.DMA
    anywhere = pl.BlockSpec(memory_space=pl.ANY)
    inputs = (rim_blocks, neighbours.T, features, tiles, theta, bias, mix)
    landed, numbers = pl.pallas_call(
        functools.partial(main_kernel, unroll=16),
        out_shape=(jax.ShapeDtypeStruct(piece, BF16), jax.ShapeDtypeStruct((blocks, LANES), I32)),
        in_specs=[anywhere] * len(inputs),
        out_specs=(anywhere, vmem),
        scratch_shapes=[
            *[pltpu.VMEM((blocks + 2 * rim, pixels, width), BF16) for _ in range(6)],
            pltpu.SMEM(rim_blocks.shape, I32),
            *[pltpu.VMEM(value.shape, value.dtype) for value in inputs[1:]],
            pltpu.SMEM((blocks, LANES), I32),
            pltpu.VMEM((blocks, pixels, width), F32),
            pltpu.VMEM(piece, F32),
            pltpu.VMEM((orders, width, width), BF16),
            pltpu.VMEM((orders, width, width), BF16),
            pltpu.VMEM((rim // 2, pixels, LANES), BF16),
            pltpu.VMEM((6, rim // 2, pixels, LANES), BF16),
            *[pltpu.VMEM(piece, BF16) for _ in range(3)],
            pltpu.VMEM((2, shells * GROUP, shells * GROUP), BF16),
            pltpu.VMEM((blocks, pixels, width), BF16),
            dma((len(inputs),)), dma, dma,
            *[dma((6,)) for _ in range(4)],
            dma((2,)), dma((2,)),
        ],
        compiler_params=pltpu.CompilerParams(
            collective_id=0, has_side_effects=True, vmem_limit_bytes=56 * 1024 * 1024
        ),
        name="filter_and_mix",
    )(*inputs)
    return pl.pallas_call(
        functools.partial(unpack_kernel, slot=neighbours.shape[1] + 1),
        out_shape=jax.ShapeDtypeStruct(features.shape, BF16),
        in_specs=[anywhere, anywhere],
        out_specs=anywhere,
        scratch_shapes=[
            pltpu.SMEM((blocks, LANES), I32),
            pltpu.VMEM(piece, BF16),
            pltpu.VMEM(features.shape, BF16),
            pltpu.VMEM(features.shape, BF16),
            dma((4,)),
            dma((5,)),
        ],
        compiler_params=pltpu.CompilerParams(vmem_limit_bytes=60 * 1024 * 1024),
        name="unpack",
    )(numbers, landed)


def solution(mesh):
    in_specs = (
        P("region", None, "shell"),
        P("region", None, None),
        P("region", None),
        P("region", None),
        P(),
        P(),
        P(),
    )
    return jax.shard_map(
        on_device, mesh=mesh, in_specs=in_specs, out_specs=P("region", None, "shell"), check_vma=False
    )
```

```python
import functools

import jax
import jax.numpy as jnp
from jax import lax
from jax.experimental import pallas as pl
from jax.experimental.pallas import tpu as pltpu
from jax.sharding import PartitionSpec as P

MESH = pl.DeviceIdType.MESH
BF16 = jnp.bfloat16
F32 = jnp.float32
I32 = jnp.int32
GROUP = 8
LANES = 128


def dot(a, b):
    return jnp.dot(a, b, preferred_element_type=F32)


def dot_nt(a, b):
    return lax.dot_general(a, b, (((1,), (1,)), ((), ())), preferred_element_type=F32)


def iota(shape, axis):
    return lax.broadcasted_iota(I32, shape, axis)


def number_blocks(near_t, rims, odd, blocks, rim):
    near_in = near_t.astype(F32).T.astype(I32)
    lane = iota((8, LANES), 1)
    rank = jnp.zeros((8, LANES), I32)
    is_rim = jnp.zeros((8, LANES), jnp.bool_)
    for row in range(2):
        first = jnp.where(odd == row, 0, rim)
        for j in range(rim):
            hit = lane == rims[row, j] + rim
            rank = rank + jnp.where(hit, first + j, 0)
            is_rim = is_rim | hit
    own = (lane >= rim) & (lane < blocks + rim)
    free = jnp.where(own & ~is_rim, 1.0, 0.0).astype(BF16)
    earlier = jnp.where(iota((LANES, LANES), 0) < iota((LANES, LANES), 1), 1.0, 0.0).astype(BF16)
    before = dot(free, earlier).astype(I32)
    position = jnp.where(is_rim, rank, 2 * rim + before)
    edge = jnp.where(lane < rim, blocks + lane + rim * odd, lane - rim * odd)
    table = jnp.where(own, position, edge)[0:1, :]

    wide = iota((blocks, LANES), 1)
    tall = iota((blocks, LANES), 0)
    table_rows = jnp.broadcast_to(table, (blocks, LANES)).astype(F32)
    found = jnp.where(wide == near_in.shape[1], tall, 0).astype(F32)
    for j in range(near_in.shape[1]):
        picked = jnp.where(near_in[:, j : j + 1] == wide, table_rows, 0.0)
        found = jnp.where(wide == j, jnp.sum(picked, axis=1, keepdims=True), found)
    gap = jnp.zeros((rim, LANES), F32)
    tail = jnp.zeros((LANES - blocks - rim, LANES), F32)
    hits = jnp.where(table == tall, 1.0, 0.0).astype(BF16)
    ordered = dot(hits, jnp.concatenate([gap, found, tail], axis=0).astype(BF16))
    where_to = jnp.sum(jnp.where(wide == tall + rim, table_rows, 0.0), axis=1, keepdims=True)
    numbers = jnp.where(wide == near_in.shape[1] + 1, where_to, ordered).astype(I32)
    top = jnp.where(wide < near_in.shape[1], blocks + 2 * rim - 1, blocks - 1)
    return jnp.clip(numbers, 0, top)


def main_kernel(
    rims_hbm, near_hbm, feat_hbm, tiles_hbm, theta_hbm, bias_hbm, mix_hbm, landed, numbers_hbm,
    e0, e1, e2, e3, e4, e5, rims, near_in, feat, tiles, theta, bias, mix, numbers_v, numbers, acc, acc_t, w0, w1,
    packed, landing, stage, arrived, mixed_out, big, third,
    input_sem, number_sem, number_out_sem, chip_send, chip_recv, cross_send, cross_recv, a2a_send, a2a_recv,
    *, unroll,
):
    n_shell = lax.axis_size("shell")
    n_region = lax.axis_size("region")
    ext = (e0, e1, e2, e3, e4, e5)
    blocks, pixels, width = feat.shape
    rim = (e0.shape[0] - blocks) // 2
    channels = theta.shape[2]
    groups = channels // GROUP
    listed = near_in.shape[0]
    me = lax.axis_index("shell")
    region = lax.axis_index("region")
    odd = lax.rem(region, 2)
    above = lax.rem(region + 1, n_region)
    below = lax.rem(region + n_region - 1, n_region)
    chip_mate = above + odd * (below - above)
    cross_mate = below + odd * (above - below)

    sources = (rims_hbm, feat_hbm, near_hbm, tiles_hbm, theta_hbm, bias_hbm, mix_hbm)
    targets = (rims, feat, near_in, tiles, theta, bias, mix)
    loads = [
        pltpu.make_async_copy(source, target, input_sem.at[n])
        for n, (source, target) in enumerate(zip(sources, targets))
    ]
    loads[0].start()
    loads[1].start()
    barrier = pltpu.get_barrier_semaphore()
    for other in (above, below):
        pl.semaphore_signal(barrier, inc=1, device_id={"region": other}, device_id_type=MESH)
    for load in loads[2:]:
        load.start()

    def greet(k, _):
        pl.semaphore_signal(
            barrier, inc=1, device_id={"shell": lax.rem(me + k, n_shell)}, device_id_type=MESH
        )
        return 0

    lax.fori_loop(1, n_shell, greet, 0)

    def pack(k):
        for p in range(rim // 2):
            packed[p] = jnp.concatenate([ext[k][p], ext[k][p + rim // 2]], axis=1)

    def unpack(k):
        for p in range(rim // 2):
            value = landing[k, p]
            ext[k][blocks + p] = value[:, :width]
            ext[k][blocks + rim // 2 + p] = value[:, width:]

    def rim_copies(k):
        cross = pltpu.make_async_remote_copy(
            src_ref=packed, dst_ref=landing.at[k],
            send_sem=cross_send.at[k], recv_sem=cross_recv.at[k],
            device_id={"region": cross_mate}, device_id_type=MESH,
        )
        chip = pltpu.make_async_remote_copy(
            src_ref=ext[k].at[pl.ds(rim, rim)], dst_ref=ext[k].at[pl.ds(blocks + rim, rim)],
            send_sem=chip_send.at[k], recv_sem=chip_recv.at[k],
            device_id={"region": chip_mate}, device_id_type=MESH,
        )
        return cross, chip

    loads[0].wait()
    loads[1].wait()
    for j in range(rim):
        e0[j] = feat[rims[odd, j]]
        e0[rim + j] = feat[rims[1 - odd, j]]
    pack(0)
    pl.semaphore_wait(barrier, n_shell + 1)
    for copy in rim_copies(0):
        copy.start()

    loads[2].wait()
    numbers_v[...] = number_blocks(near_in[...], rims, odd, blocks, rim)
    number_copy = pltpu.make_async_copy(numbers_v, numbers, number_sem)
    number_copy.start()
    number_out = pltpu.make_async_copy(numbers_v, numbers_hbm, number_out_sem)
    number_out.start()

    for load in loads[4:]:
        load.wait()
    zero = jnp.zeros((channels, channels), F32)
    for k in range(4):
        weight = theta[0, k].astype(F32)
        w0[k] = jnp.concatenate(
            [jnp.concatenate([weight, zero], axis=1), jnp.concatenate([zero, weight], axis=1)], axis=0
        ).astype(BF16)
        weight = theta[1, k].astype(F32).T
        left = jnp.concatenate([weight, zero], axis=1)
        right = jnp.concatenate([zero, weight], axis=1)
        parts = []
        for g in range(groups):
            parts += [left[g * GROUP : (g + 1) * GROUP], right[g * GROUP : (g + 1) * GROUP]]
        w1[k] = jnp.concatenate(parts, axis=0).astype(BF16)
    b0 = jnp.concatenate([bias[0:1, :], bias[0:1, :]], axis=1)

    size = big.shape[1]
    shells = mix.shape[1]

    spread = jnp.where(
        lax.shift_right_logical(iota((size, shells), 0), 3) == iota((size, shells), 1), 1.0, 0.0
    ).astype(BF16)
    same = jnp.where(
        iota((GROUP, size), 0) == lax.bitwise_and(iota((GROUP, size), 1), GROUP - 1), 1.0, 0.0
    )

    def build_mix(layer):
        rows = dot(spread, mix[layer]).astype(BF16)
        full = dot_nt(rows, spread).reshape(shells, GROUP, size)
        big[layer] = (full * same[None]).reshape(size, size).astype(BF16)

    number_copy.wait()

    def load_block(i, _):
        e0[i] = feat[numbers[i, listed]]
        return 0

    lax.fori_loop(2 * rim, blocks, load_block, 0, unroll=8)

    def product(k, i):
        parts = [ext[k][i]] + [ext[k][numbers[i, j]] for j in range(listed)]
        return dot(tiles[numbers[i, listed]], jnp.concatenate(parts, axis=0))

    def step(k, i):
        value = product(k, i)
        if k % 3 == 0:
            return value.astype(BF16)
        return (2.0 * value - ext[k - 1][i].astype(F32)).astype(BF16)

    batch = 8

    def filter_rows(orders, fresh):
        def body(q, _):
            rows = pl.ds(q * batch, batch)
            total = b0 if fresh else acc[rows].reshape(batch * pixels, width)
            for k in orders:
                total = total + dot(ext[k][rows].reshape(batch * pixels, width), w0[k])
            acc[rows] = total.reshape(batch, pixels, width)
            return 0

        lax.fori_loop(0, blocks // batch, body, 0, unroll=8)

    def filter_columns(orders, fresh):
        def body(q, _):
            rows = pl.ds(q * 4, 4)
            total = None
            for k in orders:
                term = dot_nt(w1[k], ext[3 + k][rows].reshape(4 * pixels, width))
                total = term if total is None else total + term
            for p in range(2):
                value = total[:, p * LANES : (p + 1) * LANES]
                acc_t[2 * q + p] = value if fresh else acc_t[2 * q + p] + value
            return 0

        lax.fori_loop(0, blocks // 4, body, 0, unroll=16)

    def activate(first, end):
        def body(q, _):
            rows = pl.ds(first + q * batch, batch)
            total = acc[rows].reshape(batch * pixels, width)
            total = total + dot(e3[rows].reshape(batch * pixels, width), w0[3])
            e3[rows] = jnp.maximum(total, 0.0).astype(BF16).reshape(batch, pixels, width)
            return 0

        lax.fori_loop(0, (end - first) // batch, body, 0, unroll=(end - first) // batch)

    for k in range(6):
        for copy in rim_copies(k):
            copy.wait()
        unpack(k)
        if k == 0:
            loads[3].wait()
        if k < 5:

            def body(i, _):
                ext[k + 1][i] = step(k, i)
                return 0

            cross, chip = rim_copies(k + 1)
            lax.fori_loop(0, rim, body, 0, unroll=rim)
            if k == 2:
                activate(0, rim)
            pack(k + 1)
            cross.start()
            lax.fori_loop(rim, 2 * rim, body, 0, unroll=rim)
            if k == 2:
                activate(rim, 2 * rim)
            chip.start()
            lax.fori_loop(2 * rim, blocks, body, 0, unroll=unroll)
            if k == 2:
                activate(2 * rim, blocks)
            if k == 0:
                filter_rows((0, 1), True)
            elif k == 1:
                filter_rows((2,), False)
            elif k == 2:
                build_mix(0)
            elif k == 3:
                filter_columns((0, 1), True)
            elif k == 4:
                filter_columns((2,), False)

    def a2a_send_piece(source, target, d, slot):
        pltpu.make_async_remote_copy(
            src_ref=source.at[d], dst_ref=target.at[me],
            send_sem=a2a_send.at[slot], recv_sem=a2a_recv.at[slot],
            device_id={"shell": d}, device_id_type=MESH,
        ).start()

    def finish(target, slot):
        all_but_one = target.at[pl.ds(0, n_shell - 1)]
        pltpu.make_async_copy(all_but_one, all_but_one, a2a_send.at[slot]).wait()
        pltpu.make_async_copy(all_but_one, all_but_one, a2a_recv.at[slot]).wait()

    width_of_run = 8

    def last_pieces(t, _):
        for p in range(width_of_run):
            d = lax.rem(me + 1 + t * width_of_run + p, n_shell)
            third[2 * d] = step(5, 2 * d)
            third[2 * d + 1] = step(5, 2 * d + 1)
        for p in range(width_of_run):
            d = lax.rem(me + 1 + t * width_of_run + p, n_shell)
            pair = third[pl.ds(2 * d, 2)].reshape(2 * pixels, width)
            stage[d] = (acc_t[d] + dot_nt(w1[3], pair)).astype(BF16)
        for p in range(width_of_run):
            d = lax.rem(me + 1 + t * width_of_run + p, n_shell)

            @pl.when(d != me)
            def _():
                a2a_send_piece(stage, arrived, d, 0)

        return 0

    lax.fori_loop(0, n_shell // width_of_run, last_pieces, 0)
    arrived[me] = stage[me]
    build_mix(1)
    b1 = jnp.broadcast_to(bias[1:2, :], (LANES, channels)).T
    finish(arrived, 0)

    def rows_of(g):
        return pl.ds(g * 2 * GROUP, 2 * GROUP)

    for g in range(0, groups, 2):
        x = jnp.concatenate([arrived[:, rows_of(g + p), :].reshape(size, LANES) for p in range(2)], axis=1)
        lift = jnp.concatenate([b1[(g + p) * GROUP : (g + p + 1) * GROUP] for p in range(2)], axis=1)
        total = dot(big[0], x).reshape(shells, GROUP, 2 * LANES) + lift[None]
        act = jnp.maximum(total, 0.0).reshape(size, 2 * LANES).astype(BF16)
        y = dot(big[1], act).astype(BF16)
        for p in range(2):
            part = y[:, p * LANES : (p + 1) * LANES]
            mixed_out[:, rows_of(g + p), :] = part.reshape(n_shell, 2 * GROUP, LANES)

    landed[me] = mixed_out[me]

    def send_mixed(t, _):
        a2a_send_piece(mixed_out, landed, lax.rem(me + t, n_shell), 1)
        return 0

    lax.fori_loop(1, n_shell, send_mixed, 0)
    number_out.wait()
    finish(landed, 1)


def unpack_kernel(numbers_hbm, landed, out_hbm, numbers, turned, placed, sem, load_sem, *, slot):
    blocks, pixels, width = out_hbm.shape
    number_copy = pltpu.make_async_copy(numbers_hbm, numbers, load_sem)
    number_copy.start()
    groups = width // (2 * GROUP)

    def turn(d, _):
        piece = landed[d].astype(F32)
        rows = [
            piece[(2 * g + s) * GROUP : (2 * g + s + 1) * GROUP] for s in range(2) for g in range(groups)
        ]
        value = jnp.concatenate(rows, axis=0).T.astype(BF16)
        turned[2 * d] = value[:pixels]
        turned[2 * d + 1] = value[pixels:]
        return 0

    lax.fori_loop(0, landed.shape[0], turn, 0, unroll=8)
    number_copy.wait()
    run = blocks // 4
    copies = []
    for q in range(4):

        def place(b, _):
            placed[b] = turned[numbers[b, slot]]
            return 0

        lax.fori_loop(q * run, (q + 1) * run, place, 0, unroll=8)
        rows = pl.ds(q * run, run)
        copies.append(pltpu.make_async_copy(placed.at[rows], out_hbm.at[rows], sem.at[q]))
        copies[-1].start()
    for copy in copies:
        copy.wait()


def on_device(features, tiles, neighbours, rim_blocks, theta, bias, mix):
    blocks, pixels, width = features.shape
    shells = mix.shape[1]
    n_shell = lax.axis_size("shell")
    vmem = pl.BlockSpec(memory_space=pltpu.VMEM)
    rim = rim_blocks.shape[1]
    piece = (n_shell, width, 2 * pixels)
    orders = theta.shape[1]
    dma = pltpu.SemaphoreType.DMA
    anywhere = pl.BlockSpec(memory_space=pl.ANY)
    inputs = (rim_blocks, neighbours.T, features, tiles, theta, bias, mix)
    landed, numbers = pl.pallas_call(
        functools.partial(main_kernel, unroll=48),
        out_shape=(pltpu.VMEM(piece, BF16), jax.ShapeDtypeStruct((blocks, LANES), I32)),
        in_specs=[anywhere] * len(inputs),
        out_specs=(vmem, anywhere),
        scratch_shapes=[
            *[pltpu.VMEM((blocks + 2 * rim, pixels, width), BF16) for _ in range(6)],
            pltpu.SMEM(rim_blocks.shape, I32),
            *[pltpu.VMEM(value.shape, value.dtype) for value in inputs[1:]],
            pltpu.VMEM((blocks, LANES), I32),
            pltpu.SMEM((blocks, LANES), I32),
            pltpu.VMEM((blocks, pixels, width), F32),
            pltpu.VMEM(piece, F32),
            pltpu.VMEM((orders, width, width), BF16),
            pltpu.VMEM((orders, width, width), BF16),
            pltpu.VMEM((rim // 2, pixels, LANES), BF16),
            pltpu.VMEM((6, rim // 2, pixels, LANES), BF16),
            *[pltpu.VMEM(piece, BF16) for _ in range(3)],
            pltpu.VMEM((2, shells * GROUP, shells * GROUP), BF16),
            pltpu.VMEM((blocks, pixels, width), BF16),
            dma((len(inputs),)), dma, dma,
            *[dma((6,)) for _ in range(4)],
            dma((2,)), dma((2,)),
        ],
        compiler_params=pltpu.CompilerParams(
            collective_id=0, has_side_effects=True, vmem_limit_bytes=56 * 1024 * 1024
        ),
        name="filter_and_mix",
    )(*inputs)
    return pl.pallas_call(
        functools.partial(unpack_kernel, slot=neighbours.shape[1] + 1),
        out_shape=jax.ShapeDtypeStruct(features.shape, BF16),
        in_specs=[anywhere, vmem],
        out_specs=anywhere,
        scratch_shapes=[
            pltpu.SMEM((blocks, LANES), I32),
            pltpu.VMEM(features.shape, BF16),
            pltpu.VMEM(features.shape, BF16),
            dma((4,)),
            dma,
        ],
        compiler_params=pltpu.CompilerParams(vmem_limit_bytes=16 * 1024 * 1024),
        name="unpack",
    )(numbers, landed)


def solution(mesh):
    in_specs = (
        P("region", None, "shell"),
        P("region", None, None),
        P("region", None),
        P("region", None),
        P(),
        P(),
        P(),
    )
    return jax.shard_map(
        on_device, mesh=mesh, in_specs=in_specs, out_specs=P("region", None, "shell"), check_vma=False
    )
```

```python
import functools

import jax
import jax.numpy as jnp
from jax import lax
from jax.experimental import pallas as pl
from jax.experimental.pallas import tpu as pltpu
from jax.sharding import PartitionSpec as P

MESH = pl.DeviceIdType.MESH
BF16 = jnp.bfloat16
F32 = jnp.float32
I32 = jnp.int32
GROUP = 8
LANES = 128


def dot(a, b):
    return jnp.dot(a, b, preferred_element_type=F32)


def dot_nt(a, b):
    return lax.dot_general(a, b, (((1,), (1,)), ((), ())), preferred_element_type=F32)


def iota(shape, axis):
    return lax.broadcasted_iota(I32, shape, axis)


def number_blocks(near_t, rims, odd, blocks, rim):
    near_in = near_t.astype(F32).T.astype(I32)
    lane = iota((8, LANES), 1)
    rank = jnp.zeros((8, LANES), I32)
    is_rim = jnp.zeros((8, LANES), jnp.bool_)
    for row in range(2):
        first = jnp.where(odd == row, 0, rim)
        for j in range(rim):
            hit = lane == rims[row, j] + rim
            rank = rank + jnp.where(hit, first + j, 0)
            is_rim = is_rim | hit
    own = (lane >= rim) & (lane < blocks + rim)
    free = jnp.where(own & ~is_rim, 1.0, 0.0).astype(BF16)
    earlier = jnp.where(iota((LANES, LANES), 0) < iota((LANES, LANES), 1), 1.0, 0.0).astype(BF16)
    before = dot(free, earlier).astype(I32)
    position = jnp.where(is_rim, rank, 2 * rim + before)
    edge = jnp.where(lane < rim, blocks + lane + rim * odd, lane - rim * odd)
    table = jnp.where(own, position, edge)[0:1, :]

    wide = iota((blocks, LANES), 1)
    tall = iota((blocks, LANES), 0)
    table_rows = jnp.broadcast_to(table, (blocks, LANES)).astype(F32)
    found = jnp.where(wide == near_in.shape[1], tall, 0).astype(F32)
    for j in range(near_in.shape[1]):
        picked = jnp.where(near_in[:, j : j + 1] == wide, table_rows, 0.0)
        found = jnp.where(wide == j, jnp.sum(picked, axis=1, keepdims=True), found)
    gap = jnp.zeros((rim, LANES), F32)
    tail = jnp.zeros((LANES - blocks - rim, LANES), F32)
    hits = jnp.where(table == tall, 1.0, 0.0).astype(BF16)
    ordered = dot(hits, jnp.concatenate([gap, found, tail], axis=0).astype(BF16))
    where_to = jnp.sum(jnp.where(wide == tall + rim, table_rows, 0.0), axis=1, keepdims=True)
    numbers = jnp.where(wide == near_in.shape[1] + 1, where_to, ordered).astype(I32)
    top = jnp.where(wide < near_in.shape[1], blocks + 2 * rim - 1, blocks - 1)
    return jnp.clip(numbers, 0, top)


def main_kernel(
    rims_hbm, near_hbm, feat_hbm, tiles_hbm, theta_hbm, bias_hbm, mix_hbm, out,
    e0, e1, e2, e3, e4, e5, rims, near_in, feat, tiles, theta, bias, mix, numbers_v, numbers, acc, acc_t, w0, w1,
    packed, landing, stage, arrived, mixed_out, landed, big, third,
    input_sem, number_sem, chip_send, chip_recv, cross_send, cross_recv, a2a_send, a2a_recv, run_recv,
    *, unroll,
):
    n_shell = lax.axis_size("shell")
    n_region = lax.axis_size("region")
    ext = (e0, e1, e2, e3, e4, e5)
    blocks, pixels, width = feat.shape
    rim = (e0.shape[0] - blocks) // 2
    channels = theta.shape[2]
    groups = channels // GROUP
    listed = near_in.shape[0]
    me = lax.axis_index("shell")
    region = lax.axis_index("region")
    odd = lax.rem(region, 2)
    above = lax.rem(region + 1, n_region)
    below = lax.rem(region + n_region - 1, n_region)
    chip_mate = above + odd * (below - above)
    cross_mate = below + odd * (above - below)

    sources = (rims_hbm, feat_hbm, near_hbm, tiles_hbm, theta_hbm, bias_hbm, mix_hbm)
    targets = (rims, feat, near_in, tiles, theta, bias, mix)
    loads = [
        pltpu.make_async_copy(source, target, input_sem.at[n])
        for n, (source, target) in enumerate(zip(sources, targets))
    ]
    loads[0].start()
    loads[1].start()
    barrier = pltpu.get_barrier_semaphore()
    for other in (above, below):
        pl.semaphore_signal(barrier, inc=1, device_id={"region": other}, device_id_type=MESH)
    for load in loads[2:]:
        load.start()

    def greet(k, _):
        pl.semaphore_signal(
            barrier, inc=1, device_id={"shell": lax.rem(me + k, n_shell)}, device_id_type=MESH
        )
        return 0

    lax.fori_loop(1, n_shell, greet, 0, unroll=n_shell - 1)

    def pack(k):
        for p in range(rim // 2):
            packed[p] = jnp.concatenate([ext[k][p], ext[k][p + rim // 2]], axis=1)

    def unpack(k):
        for p in range(rim // 2):
            value = landing[k, p]
            ext[k][blocks + p] = value[:, :width]
            ext[k][blocks + rim // 2 + p] = value[:, width:]

    def rim_copies(k):
        cross = pltpu.make_async_remote_copy(
            src_ref=packed, dst_ref=landing.at[k],
            send_sem=cross_send.at[k], recv_sem=cross_recv.at[k],
            device_id={"region": cross_mate}, device_id_type=MESH,
        )
        chip = pltpu.make_async_remote_copy(
            src_ref=ext[k].at[pl.ds(rim, rim)], dst_ref=ext[k].at[pl.ds(blocks + rim, rim)],
            send_sem=chip_send.at[k], recv_sem=chip_recv.at[k],
            device_id={"region": chip_mate}, device_id_type=MESH,
        )
        return cross, chip

    loads[0].wait()
    loads[1].wait()
    for j in range(rim):
        e0[j] = feat[rims[odd, j]]
        e0[rim + j] = feat[rims[1 - odd, j]]
    pack(0)
    pl.semaphore_wait(barrier, n_shell + 1)
    for copy in rim_copies(0):
        copy.start()

    loads[2].wait()
    numbers_v[...] = number_blocks(near_in[...], rims, odd, blocks, rim)
    number_copy = pltpu.make_async_copy(numbers_v, numbers, number_sem)
    number_copy.start()

    for load in loads[4:]:
        load.wait()
    zero = jnp.zeros((channels, channels), F32)
    for k in range(4):
        weight = theta[0, k].astype(F32)
        w0[k] = jnp.concatenate(
            [jnp.concatenate([weight, zero], axis=1), jnp.concatenate([zero, weight], axis=1)], axis=0
        ).astype(BF16)
        weight = theta[1, k].astype(F32).T
        left = jnp.concatenate([weight, zero], axis=1)
        right = jnp.concatenate([zero, weight], axis=1)
        parts = []
        for g in range(groups):
            parts += [left[g * GROUP : (g + 1) * GROUP], right[g * GROUP : (g + 1) * GROUP]]
        w1[k] = jnp.concatenate(parts, axis=0).astype(BF16)
    b0 = jnp.concatenate([bias[0:1, :], bias[0:1, :]], axis=1)

    size = big.shape[1]
    shells = mix.shape[1]

    spread = jnp.where(
        lax.shift_right_logical(iota((size, shells), 0), 3) == iota((size, shells), 1), 1.0, 0.0
    ).astype(BF16)
    same = jnp.where(
        iota((GROUP, size), 0) == lax.bitwise_and(iota((GROUP, size), 1), GROUP - 1), 1.0, 0.0
    )

    def build_mix(layer):
        rows = dot(spread, mix[layer]).astype(BF16)
        full = dot_nt(rows, spread).reshape(shells, GROUP, size)
        big[layer] = (full * same[None]).reshape(size, size).astype(BF16)

    number_copy.wait()

    def load_block(i, _):
        e0[i] = feat[numbers[i, listed]]
        return 0

    lax.fori_loop(2 * rim, blocks, load_block, 0, unroll=8)

    def product(k, i):
        parts = [ext[k][i]] + [ext[k][numbers[i, j]] for j in range(listed)]
        return dot(tiles[numbers[i, listed]], jnp.concatenate(parts, axis=0))

    def step(k, i):
        value = product(k, i)
        if k % 3 == 0:
            return value.astype(BF16)
        return (2.0 * value - ext[k - 1][i].astype(F32)).astype(BF16)

    batch = 8

    def filter_rows(orders, fresh):
        def body(q, _):
            rows = pl.ds(q * batch, batch)
            total = b0 if fresh else acc[rows].reshape(batch * pixels, width)
            for k in orders:
                total = total + dot(ext[k][rows].reshape(batch * pixels, width), w0[k])
            acc[rows] = total.reshape(batch, pixels, width)
            return 0

        lax.fori_loop(0, blocks // batch, body, 0, unroll=8)

    def filter_columns(orders, fresh):
        def body(q, _):
            rows = pl.ds(q * 4, 4)
            total = None
            for k in orders:
                term = dot_nt(w1[k], ext[3 + k][rows].reshape(4 * pixels, width))
                total = term if total is None else total + term
            for p in range(2):
                value = total[:, p * LANES : (p + 1) * LANES]
                acc_t[2 * q + p] = value if fresh else acc_t[2 * q + p] + value
            return 0

        lax.fori_loop(0, blocks // 4, body, 0, unroll=16)

    def activate(first, end):
        def body(q, _):
            rows = pl.ds(first + q * batch, batch)
            total = acc[rows].reshape(batch * pixels, width)
            total = total + dot(e3[rows].reshape(batch * pixels, width), w0[3])
            e3[rows] = jnp.maximum(total, 0.0).astype(BF16).reshape(batch, pixels, width)
            return 0

        lax.fori_loop(0, (end - first) // batch, body, 0, unroll=(end - first) // batch)

    for k in range(6):
        for copy in rim_copies(k):
            copy.wait()
        unpack(k)
        if k == 0:
            loads[3].wait()
        if k < 5:

            def body(i, _):
                ext[k + 1][i] = step(k, i)
                return 0

            cross, chip = rim_copies(k + 1)
            lax.fori_loop(0, rim, body, 0, unroll=rim)
            if k == 2:
                activate(0, rim)
            pack(k + 1)
            cross.start()
            lax.fori_loop(rim, 2 * rim, body, 0, unroll=rim)
            if k == 2:
                activate(rim, 2 * rim)
            chip.start()
            lax.fori_loop(2 * rim, blocks, body, 0, unroll=unroll)
            if k == 2:
                activate(2 * rim, blocks)
            if k == 0:
                filter_rows((0, 1), True)
            elif k == 1:
                filter_rows((2,), False)
            elif k == 2:
                build_mix(0)
            elif k == 3:
                filter_columns((0, 1), True)
            elif k == 4:
                filter_columns((2,), False)

    def a2a_send_piece(source, target, d, slot):
        pltpu.make_async_remote_copy(
            src_ref=source.at[d], dst_ref=target.at[me],
            send_sem=a2a_send.at[slot], recv_sem=a2a_recv.at[slot],
            device_id={"shell": d}, device_id_type=MESH,
        ).start()

    def finish(target, slot):
        all_but_one = target.at[pl.ds(0, n_shell - 1)]
        pltpu.make_async_copy(all_but_one, all_but_one, a2a_send.at[slot]).wait()
        pltpu.make_async_copy(all_but_one, all_but_one, a2a_recv.at[slot]).wait()

    width_of_run = 8

    def last_pieces(t, count):
        def target_of(p):
            return lax.rem(me + 1 + t * width_of_run + p, n_shell)

        for p in range(width_of_run):
            d = target_of(p)
            third[2 * d] = step(5, 2 * d)
            third[2 * d + 1] = step(5, 2 * d + 1)
        for p in range(width_of_run):
            d = target_of(p)
            pair = third[pl.ds(2 * d, 2)].reshape(2 * pixels, width)
            stage[d] = (acc_t[d] + dot_nt(w1[3], pair)).astype(BF16)
        for p in range(count):
            a2a_send_piece(stage, arrived, target_of(p), 0)

    def full_run(t, _):
        last_pieces(t, width_of_run)
        return 0

    runs = n_shell // width_of_run
    lax.fori_loop(0, runs - 1, full_run, 0)
    last_pieces(runs - 1, width_of_run - 1)
    arrived[me] = stage[me]
    build_mix(1)
    b1 = jnp.broadcast_to(bias[1:2, :], (LANES, channels)).T
    finish(arrived, 0)

    def rows_of(g):
        return pl.ds(g * 2 * GROUP, 2 * GROUP)

    for g in range(0, groups, 2):
        x = jnp.concatenate([arrived[:, rows_of(g + p), :].reshape(size, LANES) for p in range(2)], axis=1)
        lift = jnp.concatenate([b1[(g + p) * GROUP : (g + p + 1) * GROUP] for p in range(2)], axis=1)
        total = dot(big[0], x).reshape(shells, GROUP, 2 * LANES) + lift[None]
        act = jnp.maximum(total, 0.0).reshape(size, 2 * LANES).astype(BF16)
        y = dot(big[1], act).astype(BF16)
        for p in range(2):
            part = y[:, p * LANES : (p + 1) * LANES]
            mixed_out[:, rows_of(g + p), :] = part.reshape(n_shell, 2 * GROUP, LANES)

    landed[me] = mixed_out[me]

    def run_range(r):
        return max(1, r * width_of_run), (r + 1) * width_of_run

    def send_mixed(t, run):
        d = lax.rem(me + t, n_shell)
        pltpu.make_async_remote_copy(
            src_ref=mixed_out.at[d], dst_ref=landed.at[me],
            send_sem=a2a_send.at[1], recv_sem=run_recv.at[run],
            device_id={"shell": d}, device_id_type=MESH,
        ).start()
        return run

    for r in range(runs):
        low, high = run_range(r)
        lax.fori_loop(low, high, send_mixed, r, unroll=high - low)
    landed[me] = mixed_out[me]

    def turn(t, _):
        d = lax.rem(me + n_shell - t, n_shell)
        piece = landed[d].astype(F32)
        rows = [
            piece[(2 * g + s) * GROUP : (2 * g + s + 1) * GROUP] for s in range(2) for g in range(groups)
        ]
        value = jnp.concatenate(rows, axis=0).T.astype(BF16)
        third[2 * d] = value[:pixels]
        third[2 * d + 1] = value[pixels:]
        return 0

    for r in range(runs):
        low, high = run_range(r)
        part = landed.at[pl.ds(0, high - low)]
        pltpu.make_async_copy(part, part, run_recv.at[r]).wait()
        lax.fori_loop(r * width_of_run, high, turn, 0, unroll=width_of_run)
    sent = landed.at[pl.ds(0, n_shell - 1)]
    pltpu.make_async_copy(sent, sent, a2a_send.at[1]).wait()

    def place(b, _):
        out[b] = third[numbers[b, listed + 1]]
        return 0

    lax.fori_loop(0, blocks, place, 0, unroll=16)


def on_device(features, tiles, neighbours, rim_blocks, theta, bias, mix):
    blocks, pixels, width = features.shape
    shells = mix.shape[1]
    n_shell = lax.axis_size("shell")
    vmem = pl.BlockSpec(memory_space=pltpu.VMEM)
    rim = rim_blocks.shape[1]
    piece = (n_shell, width, 2 * pixels)
    orders = theta.shape[1]
    dma = pltpu.SemaphoreType.DMA
    anywhere = pl.BlockSpec(memory_space=pl.ANY)
    inputs = (rim_blocks, neighbours.T, features, tiles, theta, bias, mix)
    return pl.pallas_call(
        functools.partial(main_kernel, unroll=48),
        out_shape=pltpu.VMEM(features.shape, BF16),
        in_specs=[anywhere] * len(inputs),
        out_specs=vmem,
        scratch_shapes=[
            *[pltpu.VMEM((blocks + 2 * rim, pixels, width), BF16) for _ in range(6)],
            pltpu.SMEM(rim_blocks.shape, I32),
            *[pltpu.VMEM(value.shape, value.dtype) for value in inputs[1:]],
            pltpu.VMEM((blocks, LANES), I32),
            pltpu.SMEM((blocks, LANES), I32),
            pltpu.VMEM((blocks, pixels, width), F32),
            pltpu.VMEM(piece, F32),
            pltpu.VMEM((orders, width, width), BF16),
            pltpu.VMEM((orders, width, width), BF16),
            pltpu.VMEM((rim // 2, pixels, LANES), BF16),
            pltpu.VMEM((6, rim // 2, pixels, LANES), BF16),
            *[pltpu.VMEM(piece, BF16) for _ in range(4)],
            pltpu.VMEM((2, shells * GROUP, shells * GROUP), BF16),
            pltpu.VMEM((blocks, pixels, width), BF16),
            dma((len(inputs),)), dma,
            *[dma((6,)) for _ in range(4)],
            dma((2,)), dma((2,)), dma((n_shell // 8,)),
        ],
        compiler_params=pltpu.CompilerParams(
            collective_id=0, has_side_effects=True, vmem_limit_bytes=56 * 1024 * 1024
        ),
        name="filter_and_mix",
    )(*inputs)


def solution(mesh):
    in_specs = (
        P("region", None, "shell"),
        P("region", None, None),
        P("region", None),
        P("region", None),
        P(),
        P(),
        P(),
    )
    return jax.shard_map(
        on_device, mesh=mesh, in_specs=in_specs, out_specs=P("region", None, "shell"), check_vma=False
    )
```

```python
import functools

import jax
import jax.numpy as jnp
from jax import lax
from jax.experimental import pallas as pl
from jax.experimental.pallas import tpu as pltpu
from jax.sharding import PartitionSpec as P

MESH = pl.DeviceIdType.MESH
BF16 = jnp.bfloat16
F32 = jnp.float32
I32 = jnp.int32
GROUP = 8
LANES = 128


def dot(a, b):
    return jnp.dot(a, b, preferred_element_type=F32)


def dot_nt(a, b):
    return lax.dot_general(a, b, (((1,), (1,)), ((), ())), preferred_element_type=F32)


def iota(shape, axis):
    return lax.broadcasted_iota(I32, shape, axis)


def number_blocks(near_t, rims, odd, blocks, rim):
    near_in = near_t.astype(F32).T.astype(I32)
    lane = iota((8, LANES), 1)
    rank = jnp.zeros((8, LANES), I32)
    is_rim = jnp.zeros((8, LANES), jnp.bool_)
    for row in range(2):
        first = jnp.where(odd == row, 0, rim)
        for j in range(rim):
            hit = lane == rims[row, j] + rim
            rank = rank + jnp.where(hit, first + j, 0)
            is_rim = is_rim | hit
    own = (lane >= rim) & (lane < blocks + rim)
    free = jnp.where(own & ~is_rim, 1.0, 0.0).astype(BF16)
    earlier = jnp.where(iota((LANES, LANES), 0) < iota((LANES, LANES), 1), 1.0, 0.0).astype(BF16)
    before = dot(free, earlier).astype(I32)
    position = jnp.where(is_rim, rank, 2 * rim + before)
    edge = jnp.where(lane < rim, blocks + lane + rim * odd, lane - rim * odd)
    table = jnp.where(own, position, edge)[0:1, :]

    wide = iota((blocks, LANES), 1)
    tall = iota((blocks, LANES), 0)
    table_rows = jnp.broadcast_to(table, (blocks, LANES)).astype(F32)
    found = jnp.where(wide == near_in.shape[1], tall, 0).astype(F32)
    for j in range(near_in.shape[1]):
        picked = jnp.where(near_in[:, j : j + 1] == wide, table_rows, 0.0)
        found = jnp.where(wide == j, jnp.sum(picked, axis=1, keepdims=True), found)
    gap = jnp.zeros((rim, LANES), F32)
    tail = jnp.zeros((LANES - blocks - rim, LANES), F32)
    hits = jnp.where(table == tall, 1.0, 0.0).astype(BF16)
    ordered = dot(hits, jnp.concatenate([gap, found, tail], axis=0).astype(BF16))
    where_to = jnp.sum(jnp.where(wide == tall + rim, table_rows, 0.0), axis=1, keepdims=True)
    numbers = jnp.where(wide == near_in.shape[1] + 1, where_to, ordered).astype(I32)
    top = jnp.where(wide < near_in.shape[1], blocks + 2 * rim - 1, blocks - 1)
    return jnp.clip(numbers, 0, top)


def main_kernel(
    rims_hbm, near_hbm, feat_hbm, tiles_hbm, theta_hbm, bias_hbm, mix_hbm, out,
    e0, e1, e2, e3, e4, e5, rims, near_in, feat, tiles, theta, bias, mix, numbers_v, numbers, acc, acc_t, w0, w1,
    packed, landing, stage, arrived, mixed_out, landed, big, third,
    input_sem, number_sem, chip_send, chip_recv, cross_send, cross_recv, a2a_send, a2a_recv, run_recv,
    *, unroll,
):
    n_shell = lax.axis_size("shell")
    n_region = lax.axis_size("region")
    ext = (e0, e1, e2, e3, e4, e5)
    blocks, pixels, width = feat.shape
    rim = (e0.shape[0] - blocks) // 2
    channels = theta.shape[2]
    groups = channels // GROUP
    listed = near_in.shape[0]
    me = lax.axis_index("shell")
    region = lax.axis_index("region")
    odd = lax.rem(region, 2)
    above = lax.rem(region + 1, n_region)
    below = lax.rem(region + n_region - 1, n_region)
    chip_mate = above + odd * (below - above)
    cross_mate = below + odd * (above - below)

    sources = (rims_hbm, feat_hbm, near_hbm, tiles_hbm, theta_hbm, bias_hbm, mix_hbm)
    targets = (rims, feat, near_in, tiles, theta, bias, mix)
    loads = [
        pltpu.make_async_copy(source, target, input_sem.at[n])
        for n, (source, target) in enumerate(zip(sources, targets))
    ]
    loads[0].start()
    loads[1].start()
    barrier = pltpu.get_barrier_semaphore()
    for other in (above, below):
        pl.semaphore_signal(barrier, inc=1, device_id={"region": other}, device_id_type=MESH)
    for load in loads[2:]:
        load.start()

    def greet(k, _):
        pl.semaphore_signal(
            barrier, inc=1, device_id={"shell": lax.rem(me + k, n_shell)}, device_id_type=MESH
        )
        return 0

    lax.fori_loop(1, n_shell, greet, 0, unroll=n_shell - 1)

    half = rim // 2

    def pack(k, h):
        for p in range(h * half // 2, (h + 1) * half // 2):
            packed[p] = jnp.concatenate([ext[k][2 * p], ext[k][2 * p + 1]], axis=1)

    def unpack(k):
        for p in range(half):
            value = landing[k, p]
            ext[k][blocks + 2 * p] = value[:, :width]
            ext[k][blocks + 2 * p + 1] = value[:, width:]

    def rim_copies(k):
        cross = [
            pltpu.make_async_remote_copy(
                src_ref=packed.at[pl.ds(h * half // 2, half // 2)],
                dst_ref=landing.at[k, pl.ds(h * half // 2, half // 2)],
                send_sem=cross_send.at[k, h], recv_sem=cross_recv.at[k, h],
                device_id={"region": cross_mate}, device_id_type=MESH,
            )
            for h in range(2)
        ]
        chip = pltpu.make_async_remote_copy(
            src_ref=ext[k].at[pl.ds(rim, rim)], dst_ref=ext[k].at[pl.ds(blocks + rim, rim)],
            send_sem=chip_send.at[k], recv_sem=chip_recv.at[k],
            device_id={"region": chip_mate}, device_id_type=MESH,
        )
        return *cross, chip

    loads[0].wait()
    loads[1].wait()
    for j in range(rim):
        e0[j] = feat[rims[odd, j]]
        e0[rim + j] = feat[rims[1 - odd, j]]
    pack(0, 0)
    pack(0, 1)
    pl.semaphore_wait(barrier, n_shell + 1)
    for copy in rim_copies(0):
        copy.start()

    loads[2].wait()
    numbers_v[...] = number_blocks(near_in[...], rims, odd, blocks, rim)
    number_copy = pltpu.make_async_copy(numbers_v, numbers, number_sem)
    number_copy.start()

    for load in loads[4:]:
        load.wait()
    zero = jnp.zeros((channels, channels), F32)
    for k in range(4):
        weight = theta[0, k].astype(F32)
        w0[k] = jnp.concatenate(
            [jnp.concatenate([weight, zero], axis=1), jnp.concatenate([zero, weight], axis=1)], axis=0
        ).astype(BF16)
        weight = theta[1, k].astype(F32).T
        left = jnp.concatenate([weight, zero], axis=1)
        right = jnp.concatenate([zero, weight], axis=1)
        parts = []
        for g in range(groups):
            parts += [left[g * GROUP : (g + 1) * GROUP], right[g * GROUP : (g + 1) * GROUP]]
        w1[k] = jnp.concatenate(parts, axis=0).astype(BF16)
    b0 = jnp.concatenate([bias[0:1, :], bias[0:1, :]], axis=1)

    size = big.shape[1]
    shells = mix.shape[1]

    spread = jnp.where(
        lax.shift_right_logical(iota((size, shells), 0), 3) == iota((size, shells), 1), 1.0, 0.0
    ).astype(BF16)
    same = jnp.where(
        iota((GROUP, size), 0) == lax.bitwise_and(iota((GROUP, size), 1), GROUP - 1), 1.0, 0.0
    )

    def build_mix(layer):
        rows = dot(spread, mix[layer]).astype(BF16)
        full = dot_nt(rows, spread).reshape(shells, GROUP, size)
        big[layer] = (full * same[None]).reshape(size, size).astype(BF16)

    number_copy.wait()

    def load_block(i, _):
        e0[i] = feat[numbers[i, listed]]
        return 0

    lax.fori_loop(2 * rim, blocks, load_block, 0, unroll=8)

    def product(k, i):
        parts = [ext[k][i]] + [ext[k][numbers[i, j]] for j in range(listed)]
        return dot(tiles[numbers[i, listed]], jnp.concatenate(parts, axis=0))

    def step(k, i):
        value = product(k, i)
        if k % 3 == 0:
            return value.astype(BF16)
        return (2.0 * value - ext[k - 1][i].astype(F32)).astype(BF16)

    batch = 8

    def filter_rows(orders, fresh):
        def body(q, _):
            rows = pl.ds(q * batch, batch)
            total = b0 if fresh else acc[rows].reshape(batch * pixels, width)
            for k in orders:
                total = total + dot(ext[k][rows].reshape(batch * pixels, width), w0[k])
            acc[rows] = total.reshape(batch, pixels, width)
            return 0

        lax.fori_loop(0, blocks // batch, body, 0, unroll=8)

    def filter_columns(orders, fresh):
        def body(q, _):
            rows = pl.ds(q * 4, 4)
            total = None
            for k in orders:
                term = dot_nt(w1[k], ext[3 + k][rows].reshape(4 * pixels, width))
                total = term if total is None else total + term
            for p in range(2):
                value = total[:, p * LANES : (p + 1) * LANES]
                acc_t[2 * q + p] = value if fresh else acc_t[2 * q + p] + value
            return 0

        lax.fori_loop(0, blocks // 4, body, 0, unroll=16)

    def activate(first, end, batch):
        def body(q, _):
            rows = pl.ds(first + q * batch, batch)
            total = acc[rows].reshape(batch * pixels, width)
            total = total + dot(e3[rows].reshape(batch * pixels, width), w0[3])
            e3[rows] = jnp.maximum(total, 0.0).astype(BF16).reshape(batch, pixels, width)
            return 0

        lax.fori_loop(0, (end - first) // batch, body, 0, unroll=(end - first) // batch)

    for k in range(6):
        for copy in rim_copies(k):
            copy.wait()
        unpack(k)
        if k == 0:
            loads[3].wait()
        if k < 5:

            def body(i, _):
                ext[k + 1][i] = step(k, i)
                return 0

            *cross, chip = rim_copies(k + 1)
            for h in range(2):
                lax.fori_loop(h * half, (h + 1) * half, body, 0, unroll=half)
                if k == 2:
                    activate(h * half, (h + 1) * half, half)
                pack(k + 1, h)
                cross[h].start()
            lax.fori_loop(rim, 2 * rim, body, 0, unroll=rim)
            if k == 2:
                activate(rim, 2 * rim, batch)
            chip.start()
            lax.fori_loop(2 * rim, blocks, body, 0, unroll=unroll)
            if k == 2:
                activate(2 * rim, blocks, batch)
            if k == 0:
                filter_rows((0, 1), True)
            elif k == 1:
                filter_rows((2,), False)
            elif k == 2:
                build_mix(0)
            elif k == 3:
                filter_columns((0, 1), True)
            elif k == 4:
                filter_columns((2,), False)

    def a2a_send_piece(source, target, d, slot):
        pltpu.make_async_remote_copy(
            src_ref=source.at[d], dst_ref=target.at[me],
            send_sem=a2a_send.at[slot], recv_sem=a2a_recv.at[slot],
            device_id={"shell": d}, device_id_type=MESH,
        ).start()

    def finish(target, slot):
        all_but_one = target.at[pl.ds(0, n_shell - 1)]
        pltpu.make_async_copy(all_but_one, all_but_one, a2a_send.at[slot]).wait()
        pltpu.make_async_copy(all_but_one, all_but_one, a2a_recv.at[slot]).wait()

    width_of_run = 8

    def last_pieces(t, count):
        def target_of(p):
            return lax.rem(me + 1 + t * width_of_run + p, n_shell)

        for p in range(width_of_run):
            d = target_of(p)
            third[2 * d] = step(5, 2 * d)
            third[2 * d + 1] = step(5, 2 * d + 1)
        for p in range(width_of_run):
            d = target_of(p)
            pair = third[pl.ds(2 * d, 2)].reshape(2 * pixels, width)
            stage[d] = (acc_t[d] + dot_nt(w1[3], pair)).astype(BF16)
        for p in range(count):
            a2a_send_piece(stage, arrived, target_of(p), 0)

    def full_run(t, _):
        last_pieces(t, width_of_run)
        return 0

    runs = n_shell // width_of_run
    lax.fori_loop(0, runs - 1, full_run, 0)
    last_pieces(runs - 1, width_of_run - 1)
    arrived[me] = stage[me]
    build_mix(1)
    b1 = jnp.broadcast_to(bias[1:2, :], (LANES, channels)).T
    finish(arrived, 0)

    def rows_of(g):
        return pl.ds(g * 2 * GROUP, 2 * GROUP)

    for g in range(0, groups, 2):
        x = jnp.concatenate([arrived[:, rows_of(g + p), :].reshape(size, LANES) for p in range(2)], axis=1)
        lift = jnp.concatenate([b1[(g + p) * GROUP : (g + p + 1) * GROUP] for p in range(2)], axis=1)
        total = dot(big[0], x).reshape(shells, GROUP, 2 * LANES) + lift[None]
        act = jnp.maximum(total, 0.0).reshape(size, 2 * LANES).astype(BF16)
        y = dot(big[1], act).astype(BF16)
        for p in range(2):
            part = y[:, p * LANES : (p + 1) * LANES]
            mixed_out[:, rows_of(g + p), :] = part.reshape(n_shell, 2 * GROUP, LANES)

    landed[me] = mixed_out[me]

    def run_range(r):
        return max(1, r * width_of_run), (r + 1) * width_of_run

    def send_mixed(t, run):
        d = lax.rem(me + t, n_shell)
        pltpu.make_async_remote_copy(
            src_ref=mixed_out.at[d], dst_ref=landed.at[me],
            send_sem=a2a_send.at[1], recv_sem=run_recv.at[run],
            device_id={"shell": d}, device_id_type=MESH,
        ).start()
        return run

    for r in range(runs):
        low, high = run_range(r)
        lax.fori_loop(low, high, send_mixed, r, unroll=high - low)
    landed[me] = mixed_out[me]

    def turn(t, _):
        d = lax.rem(me + n_shell - t, n_shell)
        piece = landed[d].astype(F32)
        rows = [
            piece[(2 * g + s) * GROUP : (2 * g + s + 1) * GROUP] for s in range(2) for g in range(groups)
        ]
        value = jnp.concatenate(rows, axis=0).T.astype(BF16)
        third[2 * d] = value[:pixels]
        third[2 * d + 1] = value[pixels:]
        return 0

    for r in range(runs):
        low, high = run_range(r)
        part = landed.at[pl.ds(0, high - low)]
        pltpu.make_async_copy(part, part, run_recv.at[r]).wait()
        lax.fori_loop(r * width_of_run, high, turn, 0, unroll=width_of_run)
    sent = landed.at[pl.ds(0, n_shell - 1)]
    pltpu.make_async_copy(sent, sent, a2a_send.at[1]).wait()

    def place(b, _):
        out[b] = third[numbers[b, listed + 1]]
        return 0

    lax.fori_loop(0, blocks, place, 0, unroll=16)


def on_device(features, tiles, neighbours, rim_blocks, theta, bias, mix):
    blocks, pixels, width = features.shape
    shells = mix.shape[1]
    n_shell = lax.axis_size("shell")
    vmem = pl.BlockSpec(memory_space=pltpu.VMEM)
    rim = rim_blocks.shape[1]
    piece = (n_shell, width, 2 * pixels)
    orders = theta.shape[1]
    dma = pltpu.SemaphoreType.DMA
    anywhere = pl.BlockSpec(memory_space=pl.ANY)
    inputs = (rim_blocks, neighbours.T, features, tiles, theta, bias, mix)
    return pl.pallas_call(
        functools.partial(main_kernel, unroll=48),
        out_shape=pltpu.VMEM(features.shape, BF16),
        in_specs=[anywhere] * len(inputs),
        out_specs=vmem,
        scratch_shapes=[
            *[pltpu.VMEM((blocks + 2 * rim, pixels, width), BF16) for _ in range(6)],
            pltpu.SMEM(rim_blocks.shape, I32),
            *[pltpu.VMEM(value.shape, value.dtype) for value in inputs[1:]],
            pltpu.VMEM((blocks, LANES), I32),
            pltpu.SMEM((blocks, LANES), I32),
            pltpu.VMEM((blocks, pixels, width), F32),
            pltpu.VMEM(piece, F32),
            pltpu.VMEM((orders, width, width), BF16),
            pltpu.VMEM((orders, width, width), BF16),
            pltpu.VMEM((rim // 2, pixels, LANES), BF16),
            pltpu.VMEM((6, rim // 2, pixels, LANES), BF16),
            *[pltpu.VMEM(piece, BF16) for _ in range(4)],
            pltpu.VMEM((2, shells * GROUP, shells * GROUP), BF16),
            pltpu.VMEM((blocks, pixels, width), BF16),
            dma((len(inputs),)), dma,
            dma((6,)), dma((6,)), dma((6, 2)), dma((6, 2)),
            dma((2,)), dma((2,)), dma((n_shell // 8,)),
        ],
        compiler_params=pltpu.CompilerParams(
            collective_id=0, has_side_effects=True, vmem_limit_bytes=56 * 1024 * 1024
        ),
        name="filter_and_mix",
    )(*inputs)


def solution(mesh):
    in_specs = (
        P("region", None, "shell"),
        P("region", None, None),
        P("region", None),
        P("region", None),
        P(),
        P(),
        P(),
    )
    return jax.shard_map(
        on_device, mesh=mesh, in_specs=in_specs, out_specs=P("region", None, "shell"), check_vma=False
    )
```

```python
import functools

import jax
import jax.numpy as jnp
from jax import lax
from jax.experimental import pallas as pl
from jax.experimental.pallas import tpu as pltpu
from jax.sharding import PartitionSpec as P

MESH = pl.DeviceIdType.MESH
BF16 = jnp.bfloat16
F32 = jnp.float32
I32 = jnp.int32
GROUP = 8
LANES = 128


def dot(a, b):
    return jnp.dot(a, b, preferred_element_type=F32)


def dot_nt(a, b):
    return lax.dot_general(a, b, (((1,), (1,)), ((), ())), preferred_element_type=F32)


def iota(shape, axis):
    return lax.broadcasted_iota(I32, shape, axis)


def number_blocks(near_t, rims, odd, blocks, rim):
    near_in = near_t.astype(F32).T.astype(I32)
    lane = iota((8, LANES), 1)
    rank = jnp.zeros((8, LANES), I32)
    is_rim = jnp.zeros((8, LANES), jnp.bool_)
    for row in range(2):
        first = jnp.where(odd == row, 0, rim)
        for j in range(rim):
            hit = lane == rims[row, j] + rim
            rank = rank + jnp.where(hit, first + j, 0)
            is_rim = is_rim | hit
    own = (lane >= rim) & (lane < blocks + rim)
    free = jnp.where(own & ~is_rim, 1.0, 0.0).astype(BF16)
    earlier = jnp.where(iota((LANES, LANES), 0) < iota((LANES, LANES), 1), 1.0, 0.0).astype(BF16)
    before = dot(free, earlier).astype(I32)
    position = jnp.where(is_rim, rank, 2 * rim + before)
    edge = jnp.where(lane < rim, blocks + lane + rim * odd, lane - rim * odd)
    table = jnp.where(own, position, edge)[0:1, :]

    wide = iota((blocks, LANES), 1)
    tall = iota((blocks, LANES), 0)
    table_rows = jnp.broadcast_to(table, (blocks, LANES)).astype(F32)
    found = jnp.where(wide == near_in.shape[1], tall, 0).astype(F32)
    for j in range(near_in.shape[1]):
        picked = jnp.where(near_in[:, j : j + 1] == wide, table_rows, 0.0)
        found = jnp.where(wide == j, jnp.sum(picked, axis=1, keepdims=True), found)
    gap = jnp.zeros((rim, LANES), F32)
    tail = jnp.zeros((LANES - blocks - rim, LANES), F32)
    hits = jnp.where(table == tall, 1.0, 0.0).astype(BF16)
    ordered = dot(hits, jnp.concatenate([gap, found, tail], axis=0).astype(BF16))
    where_to = jnp.sum(jnp.where(wide == tall + rim, table_rows, 0.0), axis=1, keepdims=True)
    numbers = jnp.where(wide == near_in.shape[1] + 1, where_to, ordered).astype(I32)
    top = jnp.where(wide < near_in.shape[1], blocks + 2 * rim - 1, blocks - 1)
    return jnp.clip(numbers, 0, top)


def main_kernel(
    rims_hbm, near_hbm, feat_hbm, tiles_hbm, theta_hbm, bias_hbm, mix_hbm, out,
    e0, e1, e2, e3, e4, e5, rims, near_in, feat, tiles, theta, bias, mix, numbers_v, numbers, acc, acc_t, w0, w1,
    packed, landing, stage, arrived, mixed_out, landed, big, third,
    input_sem, number_sem, chip_send, chip_recv, cross_send, cross_recv, a2a_send, a2a_recv, run_recv,
    *, unroll,
):
    n_shell = lax.axis_size("shell")
    n_region = lax.axis_size("region")
    ext = (e0, e1, e2, e3, e4, e5)
    blocks, pixels, width = feat.shape
    rim = (e0.shape[0] - blocks) // 2
    channels = theta.shape[2]
    groups = channels // GROUP
    listed = near_in.shape[0]
    me = lax.axis_index("shell")
    region = lax.axis_index("region")
    odd = lax.rem(region, 2)
    above = lax.rem(region + 1, n_region)
    below = lax.rem(region + n_region - 1, n_region)
    chip_mate = above + odd * (below - above)
    cross_mate = below + odd * (above - below)

    sources = (rims_hbm, feat_hbm, near_hbm, tiles_hbm, theta_hbm, bias_hbm, mix_hbm)
    targets = (rims, feat, near_in, tiles, theta, bias, mix)
    loads = [
        pltpu.make_async_copy(source, target, input_sem.at[n])
        for n, (source, target) in enumerate(zip(sources, targets))
    ]
    loads[0].start()
    loads[1].start()
    barrier = pltpu.get_barrier_semaphore()
    for other in (above, below):
        pl.semaphore_signal(barrier, inc=1, device_id={"region": other}, device_id_type=MESH)
    for load in loads[2:]:
        load.start()

    def greet(k, _):
        pl.semaphore_signal(
            barrier, inc=1, device_id={"shell": lax.rem(me + k, n_shell)}, device_id_type=MESH
        )
        return 0

    lax.fori_loop(1, n_shell, greet, 0, unroll=n_shell - 1)

    half = rim // 2

    def pack(k, h):
        for p in range(h * half // 2, (h + 1) * half // 2):
            packed[p] = jnp.concatenate([ext[k][2 * p], ext[k][2 * p + 1]], axis=1)

    def unpack(k, h):
        for p in range(h * half // 2, (h + 1) * half // 2):
            value = landing[k, p]
            ext[k][blocks + 2 * p] = value[:, :width]
            ext[k][blocks + 2 * p + 1] = value[:, width:]

    def rim_copies(k):
        cross = [
            pltpu.make_async_remote_copy(
                src_ref=packed.at[pl.ds(h * half // 2, half // 2)],
                dst_ref=landing.at[k, pl.ds(h * half // 2, half // 2)],
                send_sem=cross_send.at[k, h], recv_sem=cross_recv.at[k, h],
                device_id={"region": cross_mate}, device_id_type=MESH,
            )
            for h in range(2)
        ]
        chip = pltpu.make_async_remote_copy(
            src_ref=ext[k].at[pl.ds(rim, rim)], dst_ref=ext[k].at[pl.ds(blocks + rim, rim)],
            send_sem=chip_send.at[k], recv_sem=chip_recv.at[k],
            device_id={"region": chip_mate}, device_id_type=MESH,
        )
        return *cross, chip

    loads[0].wait()
    loads[1].wait()
    for j in range(rim):
        e0[j] = feat[rims[odd, j]]
        e0[rim + j] = feat[rims[1 - odd, j]]
    pack(0, 0)
    pack(0, 1)
    pl.semaphore_wait(barrier, n_shell + 1)
    for copy in rim_copies(0):
        copy.start()

    loads[2].wait()
    numbers_v[...] = number_blocks(near_in[...], rims, odd, blocks, rim)
    number_copy = pltpu.make_async_copy(numbers_v, numbers, number_sem)
    number_copy.start()

    for load in loads[4:]:
        load.wait()
    zero = jnp.zeros((channels, channels), F32)
    for k in range(4):
        weight = theta[0, k].astype(F32)
        w0[k] = jnp.concatenate(
            [jnp.concatenate([weight, zero], axis=1), jnp.concatenate([zero, weight], axis=1)], axis=0
        ).astype(BF16)
        weight = theta[1, k].astype(F32).T
        left = jnp.concatenate([weight, zero], axis=1)
        right = jnp.concatenate([zero, weight], axis=1)
        parts = []
        for g in range(groups):
            parts += [left[g * GROUP : (g + 1) * GROUP], right[g * GROUP : (g + 1) * GROUP]]
        w1[k] = jnp.concatenate(parts, axis=0).astype(BF16)
    b0 = jnp.concatenate([bias[0:1, :], bias[0:1, :]], axis=1)

    size = big.shape[1]
    shells = mix.shape[1]

    spread = jnp.where(
        lax.shift_right_logical(iota((size, shells), 0), 3) == iota((size, shells), 1), 1.0, 0.0
    ).astype(BF16)
    same = jnp.where(
        iota((GROUP, size), 0) == lax.bitwise_and(iota((GROUP, size), 1), GROUP - 1), 1.0, 0.0
    )

    def build_mix(layer):
        rows = dot(spread, mix[layer]).astype(BF16)
        full = dot_nt(rows, spread).reshape(shells, GROUP, size)
        big[layer] = (full * same[None]).reshape(size, size).astype(BF16)

    number_copy.wait()

    def load_block(i, _):
        e0[i] = feat[numbers[i, listed]]
        return 0

    lax.fori_loop(2 * rim, blocks, load_block, 0, unroll=8)

    def product(k, i):
        parts = [ext[k][i]] + [ext[k][numbers[i, j]] for j in range(listed)]
        return dot(tiles[numbers[i, listed]], jnp.concatenate(parts, axis=0))

    def step(k, i):
        value = product(k, i)
        if k % 3 == 0:
            return value.astype(BF16)
        return (2.0 * value - ext[k - 1][i].astype(F32)).astype(BF16)

    batch = 8

    def filter_rows(orders, fresh):
        def body(q, _):
            rows = pl.ds(q * batch, batch)
            total = b0 if fresh else acc[rows].reshape(batch * pixels, width)
            for k in orders:
                total = total + dot(ext[k][rows].reshape(batch * pixels, width), w0[k])
            acc[rows] = total.reshape(batch, pixels, width)
            return 0

        lax.fori_loop(0, blocks // batch, body, 0, unroll=8)

    def filter_columns(orders, fresh):
        def body(q, _):
            rows = pl.ds(q * 4, 4)
            total = None
            for k in orders:
                term = dot_nt(w1[k], ext[3 + k][rows].reshape(4 * pixels, width))
                total = term if total is None else total + term
            for p in range(2):
                value = total[:, p * LANES : (p + 1) * LANES]
                acc_t[2 * q + p] = value if fresh else acc_t[2 * q + p] + value
            return 0

        lax.fori_loop(0, blocks // 4, body, 0, unroll=16)

    def activate(first, end, batch):
        def body(q, _):
            rows = pl.ds(first + q * batch, batch)
            total = acc[rows].reshape(batch * pixels, width)
            total = total + dot(e3[rows].reshape(batch * pixels, width), w0[3])
            e3[rows] = jnp.maximum(total, 0.0).astype(BF16).reshape(batch, pixels, width)
            return 0

        lax.fori_loop(0, (end - first) // batch, body, 0, unroll=(end - first) // batch)

    for k in range(6):
        *cross, chip = rim_copies(k)
        chip.wait()
        for h in range(2):
            cross[h].wait()
            unpack(k, h)
        if k == 0:
            loads[3].wait()
        if k < 5:

            def body(i, _):
                ext[k + 1][i] = step(k, i)
                return 0

            *cross, chip = rim_copies(k + 1)
            for h in range(2):
                lax.fori_loop(h * half, (h + 1) * half, body, 0, unroll=half)
                if k == 2:
                    activate(h * half, (h + 1) * half, half)
                pack(k + 1, h)
                cross[h].start()
            lax.fori_loop(rim, 2 * rim, body, 0, unroll=rim)
            if k == 2:
                activate(rim, 2 * rim, batch)
            chip.start()
            lax.fori_loop(2 * rim, blocks, body, 0, unroll=unroll)
            if k == 2:
                activate(2 * rim, blocks, batch)
            if k == 0:
                filter_rows((0, 1), True)
            elif k == 1:
                filter_rows((2,), False)
            elif k == 2:
                build_mix(0)
            elif k == 3:
                filter_columns((0, 1), True)
            elif k == 4:
                filter_columns((2,), False)

    def a2a_send_piece(source, target, d, slot):
        pltpu.make_async_remote_copy(
            src_ref=source.at[d], dst_ref=target.at[me],
            send_sem=a2a_send.at[slot], recv_sem=a2a_recv.at[slot],
            device_id={"shell": d}, device_id_type=MESH,
        ).start()

    def finish(target, slot):
        all_but_one = target.at[pl.ds(0, n_shell - 1)]
        pltpu.make_async_copy(all_but_one, all_but_one, a2a_send.at[slot]).wait()
        pltpu.make_async_copy(all_but_one, all_but_one, a2a_recv.at[slot]).wait()

    width_of_run = 8

    def last_pieces(t, count):
        def target_of(p):
            return lax.rem(me + 1 + t * width_of_run + p, n_shell)

        for p in range(width_of_run):
            d = target_of(p)
            third[2 * d] = step(5, 2 * d)
            third[2 * d + 1] = step(5, 2 * d + 1)
        for p in range(width_of_run):
            d = target_of(p)
            pair = third[pl.ds(2 * d, 2)].reshape(2 * pixels, width)
            stage[d] = (acc_t[d] + dot_nt(w1[3], pair)).astype(BF16)
        for p in range(count):
            a2a_send_piece(stage, arrived, target_of(p), 0)

    def full_run(t, _):
        last_pieces(t, width_of_run)
        return 0

    runs = n_shell // width_of_run
    lax.fori_loop(0, runs - 1, full_run, 0)
    last_pieces(runs - 1, width_of_run - 1)
    arrived[me] = stage[me]
    build_mix(1)
    b1 = jnp.broadcast_to(bias[1:2, :], (LANES, channels)).T
    finish(arrived, 0)

    def rows_of(g):
        return pl.ds(g * 2 * GROUP, 2 * GROUP)

    for g in range(0, groups, 4):
        x = jnp.concatenate([arrived[:, rows_of(g + p), :].reshape(size, LANES) for p in range(4)], axis=1)
        lift = jnp.concatenate([b1[(g + p) * GROUP : (g + p + 1) * GROUP] for p in range(4)], axis=1)
        total = dot(big[0], x).reshape(shells, GROUP, 4 * LANES) + lift[None]
        act = jnp.maximum(total, 0.0).reshape(size, 4 * LANES).astype(BF16)
        y = dot(big[1], act).astype(BF16)
        for p in range(4):
            part = y[:, p * LANES : (p + 1) * LANES]
            mixed_out[:, rows_of(g + p), :] = part.reshape(n_shell, 2 * GROUP, LANES)

    landed[me] = mixed_out[me]

    def run_range(r):
        return max(1, r * width_of_run), (r + 1) * width_of_run

    def send_mixed(t, run):
        d = lax.rem(me + t, n_shell)
        pltpu.make_async_remote_copy(
            src_ref=mixed_out.at[d], dst_ref=landed.at[me],
            send_sem=a2a_send.at[1], recv_sem=run_recv.at[run],
            device_id={"shell": d}, device_id_type=MESH,
        ).start()
        return run

    for r in range(runs):
        low, high = run_range(r)
        lax.fori_loop(low, high, send_mixed, r, unroll=high - low)
    landed[me] = mixed_out[me]

    def turn(t, _):
        d = lax.rem(me + n_shell - t, n_shell)
        piece = landed[d].astype(F32)
        rows = [
            piece[(2 * g + s) * GROUP : (2 * g + s + 1) * GROUP] for s in range(2) for g in range(groups)
        ]
        value = jnp.concatenate(rows, axis=0).T.astype(BF16)
        third[2 * d] = value[:pixels]
        third[2 * d + 1] = value[pixels:]
        return 0

    for r in range(runs):
        low, high = run_range(r)
        part = landed.at[pl.ds(0, high - low)]
        pltpu.make_async_copy(part, part, run_recv.at[r]).wait()
        lax.fori_loop(r * width_of_run, high, turn, 0, unroll=width_of_run)
    sent = landed.at[pl.ds(0, n_shell - 1)]
    pltpu.make_async_copy(sent, sent, a2a_send.at[1]).wait()

    def place(b, _):
        out[b] = third[numbers[b, listed + 1]]
        return 0

    lax.fori_loop(0, blocks, place, 0, unroll=16)


def on_device(features, tiles, neighbours, rim_blocks, theta, bias, mix):
    blocks, pixels, width = features.shape
    shells = mix.shape[1]
    n_shell = lax.axis_size("shell")
    vmem = pl.BlockSpec(memory_space=pltpu.VMEM)
    rim = rim_blocks.shape[1]
    piece = (n_shell, width, 2 * pixels)
    orders = theta.shape[1]
    dma = pltpu.SemaphoreType.DMA
    anywhere = pl.BlockSpec(memory_space=pl.ANY)
    inputs = (rim_blocks, neighbours.T, features, tiles, theta, bias, mix)
    return pl.pallas_call(
        functools.partial(main_kernel, unroll=48),
        out_shape=pltpu.VMEM(features.shape, BF16),
        in_specs=[anywhere] * len(inputs),
        out_specs=vmem,
        scratch_shapes=[
            *[pltpu.VMEM((blocks + 2 * rim, pixels, width), BF16) for _ in range(6)],
            pltpu.SMEM(rim_blocks.shape, I32),
            *[pltpu.VMEM(value.shape, value.dtype) for value in inputs[1:]],
            pltpu.VMEM((blocks, LANES), I32),
            pltpu.SMEM((blocks, LANES), I32),
            pltpu.VMEM((blocks, pixels, width), F32),
            pltpu.VMEM(piece, F32),
            pltpu.VMEM((orders, width, width), BF16),
            pltpu.VMEM((orders, width, width), BF16),
            pltpu.VMEM((rim // 2, pixels, LANES), BF16),
            pltpu.VMEM((6, rim // 2, pixels, LANES), BF16),
            *[pltpu.VMEM(piece, BF16) for _ in range(4)],
            pltpu.VMEM((2, shells * GROUP, shells * GROUP), BF16),
            pltpu.VMEM((blocks, pixels, width), BF16),
            dma((len(inputs),)), dma,
            dma((6,)), dma((6,)), dma((6, 2)), dma((6, 2)),
            dma((2,)), dma((2,)), dma((n_shell // 8,)),
        ],
        compiler_params=pltpu.CompilerParams(
            collective_id=0, has_side_effects=True, vmem_limit_bytes=56 * 1024 * 1024
        ),
        name="filter_and_mix",
    )(*inputs)


def solution(mesh):
    in_specs = (
        P("region", None, "shell"),
        P("region", None, None),
        P("region", None),
        P("region", None),
        P(),
        P(),
        P(),
    )
    return jax.shard_map(
        on_device, mesh=mesh, in_specs=in_specs, out_specs=P("region", None, "shell"), check_vma=False
    )
```
